32 devices in a mesh: groups: 2 (over x), ctx: 16 (over z, y, core).
Axes of the slice: x: 2, y: 2, z: 4, core: 2. Of those that a mesh axis runs over, the one named last changes fastest.
Arguments:
- queries: bfloat16 [8192, 2560], P(('groups', 'ctx')), parts along dimension 0, may hold values from -22 to 22
- answer_keys: bfloat16 [8192, 512], P(('groups', 'ctx')), parts along dimension 0, may hold values from -15 to 15
- answer_values: bfloat16 [8192, 512], P(('groups', 'ctx')), parts along dimension 0, may hold values from -6 to 6
- prompt_keys: bfloat16 [128, 512], P(('groups', 'ctx')), parts along dimension 0, may hold values from -15 to 15
- prompt_values: bfloat16 [128, 512], P(('groups', 'ctx')), parts along dimension 0, may hold values from -6 to 6
- positions: int32 [8192], P(('groups', 'ctx')), parts along dimension 0, may hold values from 64 to 1087, as said below
- ancestry: int32 [32, 16], P(('groups', 'ctx')), parts along dimension 0, may hold values from 0 to 1, as said below
- out_grad: bfloat16 [8192, 2560], P(('groups', 'ctx')), parts along dimension 0, may hold values from -6 to 6
Outputs:
- attended: bfloat16 [8192, 2560], P(('groups', 'ctx')), parts along dimension 0
- grad_queries: bfloat16 [8192, 2560], P(('groups', 'ctx')), parts along dimension 0
- grad_keys: bfloat16 [8192, 512], P(('groups', 'ctx')), parts along dimension 0
- grad_values: bfloat16 [8192, 512], P(('groups', 'ctx')), parts along dimension 0
- grad_prompt_keys: bfloat16 [128, 512], P(('groups', 'ctx')), parts along dimension 0
- grad_prompt_values: bfloat16 [128, 512], P(('groups', 'ctx')), parts along dimension 0
The draws below stay inside these ranges and needn't reach their ends.
There are 2 independent parts, one for each index of `groups`. The reference program is written for one: setup_inputs(seed, part) draws one part's arguments, and reference() takes and returns one part's arrays. A program takes and returns all parts, laid end to end along the dimension named above; each array names one. Nothing has to cross between parts.
Inputs may be any that keep to these rules, and one draw needn't show every extreme that they name: Tree tokens are packed in blocks of 256, parents before children, one branch a block. ancestry[b, c] is 1 exactly when block c is block b or an ancestor of it. Every ancestor of a block lies among the 3 blocks before it; in every draw block 3 descends from block 0 through every block between. `positions`: A token's position is 64 plus the number of its ancestor tokens in the tree.
All inputs are finite; a program needn't handle non-finite values.
Results may differ from the reference program's by a relative error of at most 0.0085.
The reference program's roundings to bfloat16 on the way (of `q_rot`, `k_rot`, `pk_rot`, `weights` and `dscores`) count: a program that leaves them out, or rounds other values in their place, can miss the bound.
Values may be sent and summed in bfloat16 or wider, within the bound.
No kernel may reach another device: no remote copies, remote signals or barrier semaphores. Data moves between devices by JAX's collectives and lax.ppermute only.
A program may use at most 64 MiB of HBM per device.

```python
import jax
import jax.numpy as jnp
from jax import lax

QH = 20
KVH = 4
HD = 128
TOK_DEV = 256
SPAN = 4
TOKENS = 4096
PROMPT = 64
NBLK = 16


def draw_rows(key, rows, cols):
    return jnp.clip(jax.random.normal(key, (rows, cols), jnp.float32), -6.0, 6.0)


def draw_queries(key, part):
    return draw_rows(key, TOKENS, QH * HD).astype(jnp.bfloat16)


def draw_answer_keys(key, part):
    return draw_rows(key, TOKENS, KVH * HD).astype(jnp.bfloat16)


def draw_prompt_keys(key, part):
    return draw_rows(key, PROMPT, KVH * HD).astype(jnp.bfloat16)


def build_tree(key):
    base = jax.random.fold_in(key, 11)
    follow = jax.random.randint(jax.random.fold_in(base, 1), (NBLK,), 0, 4, dtype=jnp.int32)
    rooted = jax.random.randint(jax.random.fold_in(base, 2), (NBLK,), 0, 4, dtype=jnp.int32)
    ranks = jax.random.randint(jax.random.fold_in(base, 3), (NBLK, NBLK), 0, 65536, dtype=jnp.int32)
    index = jnp.arange(NBLK, dtype=jnp.int32)

    def place(block, state):
        table, lowest = state
        reach = block - SPAN + 1
        eligible = (index < block) & (index >= reach) & (lowest >= reach)
        ranked = jnp.where(eligible, ranks[block] * NBLK + index, -1)
        best = jnp.argmax(ranked).astype(jnp.int32)
        has_any = jnp.max(ranked) >= 0
        prev_ok = jnp.any(eligible & (index == block - 1))
        parent = jnp.where(rooted[block] == 0, -1, best)
        parent = jnp.where(has_any, parent, -1)
        parent = jnp.where(prev_ok & (follow[block] < 2), block - 1, parent)
        parent = jnp.where(block < SPAN, block - 1, parent).astype(jnp.int32)
        safe = jnp.maximum(parent, 0)
        row = jnp.where(parent >= 0, table[safe], 0)
        row = jnp.where(index == block, 1, row).astype(jnp.int32)
        table = table.at[block].set(row)
        lowest = lowest.at[block].set(jnp.where(parent >= 0, lowest[safe], block).astype(jnp.int32))
        return (table, lowest)
    table, lowest = lax.fori_loop(0, NBLK, place, (jnp.zeros((NBLK, NBLK), jnp.int32), index))
    depth = jnp.sum(table, axis=1) - 1
    places = PROMPT + jnp.repeat(depth * TOK_DEV, TOK_DEV) + jnp.tile(jnp.arange(TOK_DEV, dtype=jnp.int32), NBLK)
    return (table.astype(jnp.int32), places.astype(jnp.int32))


def draw_positions(key, part):
    return build_tree(key)[1]


def draw_ancestry(key, part):
    return build_tree(key)[0]


def steps_of(rng, dims, cuts, least, top_value):
    loudness = 1.0
    for dim, shards_of in cuts:
        heights = jax.random.uniform(jax.random.fold_in(jax.random.fold_in(rng, 6), dim), (shards_of,), jnp.float32, least / len(cuts), top_value / len(cuts))
        loudness = loudness * jnp.repeat(jnp.exp(heights), dims[dim] // shards_of).reshape((-1,) + (1,) * (len(dims) - 1 - dim))
    return loudness


def bell_draw(own_key, extent, scale, bound, shards=(), kind=jnp.bfloat16):
    factor_of = steps_of(own_key, extent, shards, -0.22, 0.18) if shards else 1.0
    values = jax.random.normal(own_key, extent, jnp.float32) * scale * factor_of
    return jnp.minimum(jnp.maximum(values, -bound), bound).astype(kind)


def setup_inputs(seed: int = 0, part: int = 0) -> dict:
    key_list = jax.random.split(jax.random.key(seed), 9)
    part_keys = jax.random.split(jax.random.fold_in(key_list[8], part), 9)
    return {
        "queries": draw_queries(jax.random.fold_in(jax.random.fold_in(key_list[8], part), 71), part),
        "answer_keys": draw_answer_keys(jax.random.fold_in(jax.random.fold_in(key_list[8], part), 71), part),
        "answer_values": bell_draw(part_keys[2], (TOKENS, KVH * HD), 1.0, 6.0, ((0, 16),)),
        "prompt_keys": draw_prompt_keys(jax.random.fold_in(jax.random.fold_in(key_list[8], part), 71), part),
        "prompt_values": bell_draw(part_keys[4], (PROMPT, KVH * HD), 1.0, 6.0, ((0, 16),)),
        "positions": draw_positions(jax.random.fold_in(jax.random.fold_in(key_list[8], part), 71), part),
        "ancestry": draw_ancestry(jax.random.fold_in(jax.random.fold_in(key_list[8], part), 71), part),
        "out_grad": bell_draw(part_keys[7], (TOKENS, QH * HD), 1.0, 6.0, ((0, 16),)),
    }


rope_base = 1000000.0


def rotate(values, places, sign):
    rows = values.shape[0]
    split = values.astype(jnp.float32).reshape(rows, -1, HD)
    half = HD // 2
    freqs = rope_base ** (-(2.0 * jnp.arange(half, dtype=jnp.float32)) / HD)
    angles = places.astype(jnp.float32)[:, None] * freqs[None, :]
    cosine = jnp.cos(angles)[:, None, :]
    sine = sign * jnp.sin(angles)[:, None, :]
    first = split[..., :half]
    second = split[..., half:]
    joined = jnp.concatenate([first * cosine - second * sine, second * cosine + first * sine], axis=-1)
    return joined.reshape(rows, -1)


def head_scores(head_q, head_k, visible):
    scores = jnp.einsum("tgd,kd->gtk", head_q.astype(jnp.float32), head_k.astype(jnp.float32)) * (HD ** -0.5)
    return jnp.where(visible[None], scores, -jnp.inf)


def head_forward(head_q, head_k, head_v, visible):
    scores = head_scores(head_q, head_k, visible)
    peak = jnp.max(scores, axis=-1, keepdims=True)
    log_total = peak + jnp.log(jnp.sum(jnp.exp(scores - peak), axis=-1, keepdims=True))
    weights = jnp.exp(scores - log_total).astype(jnp.bfloat16)
    mixed = jnp.einsum("gtk,kd->tgd", weights.astype(jnp.float32), head_v.astype(jnp.float32)).astype(jnp.bfloat16)
    return mixed, log_total[..., 0]


def head_backward(head_q, head_k, head_v, visible, head_g, mixed, log_total):
    scores = head_scores(head_q, head_k, visible)
    probs = jnp.exp(scores - log_total[..., None])
    weights = probs.astype(jnp.bfloat16)
    delta = jnp.sum(head_g.astype(jnp.float32) * mixed.astype(jnp.float32), axis=-1)
    dweights = jnp.einsum("tgd,kd->gtk", head_g.astype(jnp.float32), head_v.astype(jnp.float32))
    dscores = (probs * (dweights - jnp.transpose(delta)[..., None]) * (HD ** -0.5)).astype(jnp.bfloat16)
    grad_v = jnp.einsum("gtk,tgd->kd", weights.astype(jnp.float32), head_g.astype(jnp.float32))
    grad_q = jnp.einsum("gtk,kd->tgd", dscores.astype(jnp.float32), head_k.astype(jnp.float32))
    grad_k = jnp.einsum("gtk,tgd->kd", dscores.astype(jnp.float32), head_q.astype(jnp.float32))
    return grad_q, grad_k, grad_v


def split_query(values):
    rows = values.shape[0]
    return values.reshape(rows, KVH, QH // KVH, HD).transpose(1, 0, 2, 3)


def split_key(values):
    rows = values.shape[0]
    return values.reshape(rows, KVH, HD).transpose(1, 0, 2)


def attend_block(q_rot, keys, vals, visible, grads):
    rows = q_rot.shape[0]
    count = keys.shape[0]
    heads_q = split_query(q_rot)
    heads_k = split_key(keys)
    heads_v = split_key(vals)
    heads_g = split_query(grads)
    mixed, log_total = lax.map(lambda group: head_forward(group[0], group[1], group[2], visible), (heads_q, heads_k, heads_v))
    grad_q, grad_k, grad_v = lax.map(lambda group: head_backward(group[0], group[1], group[2], visible, group[3], group[4], group[5]), (heads_q, heads_k, heads_v, heads_g, mixed, log_total))
    attended = mixed.transpose(1, 0, 2, 3).reshape(rows, QH * HD)
    grad_q = grad_q.transpose(1, 0, 2, 3).reshape(rows, QH * HD)
    grad_k = grad_k.transpose(1, 0, 2).reshape(count, KVH * HD)
    grad_v = grad_v.transpose(1, 0, 2).reshape(count, KVH * HD)
    return attended, grad_q, grad_k, grad_v


def reference(queries, answer_keys, answer_values, prompt_keys, prompt_values, positions, ancestry, out_grad):
    q_rot = rotate(queries, positions, 1.0).astype(jnp.bfloat16)
    k_rot = rotate(answer_keys, positions, 1.0).astype(jnp.bfloat16)
    prompt_places = jnp.arange(PROMPT, dtype=jnp.int32)
    pk_rot = rotate(prompt_keys, prompt_places, 1.0).astype(jnp.bfloat16)
    width = KVH * HD
    padding = (SPAN - 1) * TOK_DEV
    k_pad = jnp.concatenate([jnp.zeros((padding, width), jnp.bfloat16), k_rot], axis=0)
    v_pad = jnp.concatenate([jnp.zeros((padding, width), jnp.bfloat16), answer_values], axis=0)
    lower = jnp.arange(TOK_DEV, dtype=jnp.int32)[None, :] <= jnp.arange(TOK_DEV, dtype=jnp.int32)[:, None]
    slot_ids = jnp.arange(SPAN, dtype=jnp.int32)
    own_slot = slot_ids == SPAN - 1

    def visit(state, block):
        acc_k, acc_v, prompt_acc_k, prompt_acc_v = state
        base = block * TOK_DEV
        block_q = lax.dynamic_slice_in_dim(q_rot, base, TOK_DEV, 0)
        block_g = lax.dynamic_slice_in_dim(out_grad, base, TOK_DEV, 0)
        window_k = lax.dynamic_slice_in_dim(k_pad, base, SPAN * TOK_DEV, 0)
        window_v = lax.dynamic_slice_in_dim(v_pad, base, SPAN * TOK_DEV, 0)
        blocks_in = block - (SPAN - 1) + slot_ids
        table = lax.dynamic_index_in_dim(ancestry, block, 0, False)
        seen = jnp.where(blocks_in >= 0, table[jnp.clip(blocks_in, 0, NBLK - 1)], 0) > 0
        window_seen = seen[None, :, None] & (jnp.logical_not(own_slot)[None, :, None] | lower[:, None, :])
        visible = jnp.concatenate([jnp.ones((TOK_DEV, PROMPT), bool), window_seen.reshape(TOK_DEV, SPAN * TOK_DEV)], axis=1)
        keys = jnp.concatenate([pk_rot, window_k], axis=0)
        vals = jnp.concatenate([prompt_values, window_v], axis=0)
        attended, grad_q, grad_k, grad_v = attend_block(block_q, keys, vals, visible, block_g)
        acc_k = lax.dynamic_update_slice_in_dim(acc_k, lax.dynamic_slice_in_dim(acc_k, base, SPAN * TOK_DEV, 0) + grad_k[PROMPT:], base, 0)
        acc_v = lax.dynamic_update_slice_in_dim(acc_v, lax.dynamic_slice_in_dim(acc_v, base, SPAN * TOK_DEV, 0) + grad_v[PROMPT:], base, 0)
        prompt_acc_k = prompt_acc_k + grad_k[:PROMPT]
        prompt_acc_v = prompt_acc_v + grad_v[:PROMPT]
        return (acc_k, acc_v, prompt_acc_k, prompt_acc_v), (attended, grad_q)

    start = (jnp.zeros((padding + TOKENS, width), jnp.float32), jnp.zeros((padding + TOKENS, width), jnp.float32),
             jnp.zeros((PROMPT, width), jnp.float32), jnp.zeros((PROMPT, width), jnp.float32))
    state, stacked = lax.scan(visit, start, jnp.arange(NBLK, dtype=jnp.int32))
    acc_k, acc_v, prompt_acc_k, prompt_acc_v = state
    attended = stacked[0].reshape(TOKENS, QH * HD)
    grad_queries = rotate(stacked[1].reshape(TOKENS, QH * HD), positions, -1.0).astype(jnp.bfloat16)
    grad_keys = rotate(acc_k[padding:], positions, -1.0).astype(jnp.bfloat16)
    grad_values = acc_v[padding:].astype(jnp.bfloat16)
    grad_prompt_keys = rotate(prompt_acc_k, prompt_places, -1.0).astype(jnp.bfloat16)
    grad_prompt_values = prompt_acc_v.astype(jnp.bfloat16)
    return (attended, grad_queries, grad_keys, grad_values, grad_prompt_keys, grad_prompt_values)
```

```python
import functools

import jax
import jax.numpy as jnp
from jax import lax
from jax.experimental import pallas as pl
from jax.experimental.pallas import tpu as pltpu
from jax.sharding import PartitionSpec as P

QH = 20
KVH = 4
GROUP = QH // KVH
HD = 128
SPAN = 4
SCALE = HD**-0.5
LOG2E = 1.4426950408889634
HIDDEN = -1e30

rope_base = 1000000.0

f32 = jnp.float32
bf16 = jnp.bfloat16


def permute(value, pairs):
    return lax.ppermute(value, "ctx", pairs)


def angle_tables(places):
    half = HD // 2
    freqs = rope_base ** (-(2.0 * jnp.arange(half, dtype=f32)) / HD)
    angles = places.astype(f32)[:, None] * freqs[None, :]
    cosine, sine = jnp.cos(angles), jnp.sin(angles)
    return jnp.concatenate([cosine, cosine], axis=1), jnp.concatenate([-sine, sine], axis=1)


def rotate(values, cosine, sine):
    rows = values.shape[0]
    split = values.astype(f32).reshape(rows, -1, HD)
    swapped = jnp.concatenate([split[..., HD // 2 :], split[..., : HD // 2]], axis=-1)
    return (split * cosine[:, None] + swapped * sine[:, None]).reshape(rows, -1)


def dot(a, b, ca, cb):
    return lax.dot_general(a, b, (((ca,), (cb,)), ((), ())), preferred_element_type=f32)


def turn(x, cosine, sine):
    return x * cosine + pltpu.roll(x, HD // 2, 1) * sine


def attend_kernel(
    seen, q_ref, g_ref, cos_ref, sin_ref, own_ref, w1_ref, w2_ref, w3_ref, pr_ref,
    o_ref, dq_ref, d0_ref, d1_ref, d2_ref, d3_ref, dp_ref,
    k_buf, v_buf, dk_buf, dv_buf,
):
    rows = q_ref.shape[0]
    width = KVH * HD
    col = pl.program_id(0) * HD
    k_at = pl.ds(pl.multiple_of(col, HD), HD)
    v_at = pl.ds(pl.multiple_of(col + width, HD), HD)
    parts = [own_ref, w1_ref, w2_ref, w3_ref, pr_ref]
    starts = [0, rows, 2 * rows, 3 * rows, 4 * rows]
    for part, start in zip(parts, starts):
        count = part.shape[0]
        k_buf[start : start + count, :] = part[:, k_at]
        v_buf[start : start + count, :] = part[:, v_at]
    k, v = k_buf[...], v_buf[...]
    cosine, sine = cos_ref[...], sin_ref[...]
    lower = lax.broadcasted_iota(jnp.int32, (rows, rows), 1) <= lax.broadcasted_iota(
        jnp.int32, (rows, rows), 0
    )
    bias = [jnp.where(seen[i] > 0, 0.0, HIDDEN).astype(f32) for i in range(3)]
    for h in range(GROUP):
        cols = slice(h * HD, (h + 1) * HD)
        q = turn(q_ref[:, cols].astype(f32), cosine, sine).astype(bf16)
        g = g_ref[:, cols]
        s = dot(q, k, 1, 1)
        s_own = jnp.where(lower, s[:, :rows], HIDDEN)
        s_win = [s[:, rows * (i + 1) : rows * (i + 2)] for i in range(3)]
        s_pr = s[:, 4 * rows :]
        peak = jnp.maximum(
            jnp.max(s_own, axis=1, keepdims=True), jnp.max(s_pr, axis=1, keepdims=True)
        )
        for i in range(3):
            peak = jnp.maximum(peak, jnp.max(s_win[i], axis=1, keepdims=True) + bias[i])
        base = peak * (SCALE * LOG2E)
        e = (
            [jnp.exp2(s_own * (SCALE * LOG2E) - base)]
            + [jnp.exp2(s_win[i] * (SCALE * LOG2E) - (base - bias[i])) for i in range(3)]
            + [jnp.exp2(s_pr * (SCALE * LOG2E) - base)]
        )
        total = sum(jnp.sum(x, axis=1, keepdims=True) for x in e)
        w = jnp.concatenate(e, axis=1) * (1.0 / total)
        wb = w.astype(bf16)
        o = dot(wb, v, 1, 0).astype(bf16)
        o_ref[:, cols] = o
        delta = jnp.sum(o.astype(f32) * g.astype(f32), axis=1, keepdims=True)
        dw = dot(g, v, 1, 1)
        ds = (w * (dw - delta) * SCALE).astype(bf16)
        dq_ref[:, cols] = turn(dot(ds, k, 1, 0), cosine, -sine).astype(bf16)
        dk, dv = dot(ds, q, 0, 0), dot(wb, g, 0, 0)
        if h == 0:
            dk_buf[...] = dk
            dv_buf[...] = dv
        else:
            dk_buf[...] += dk
            dv_buf[...] += dv
    outs = [d0_ref, d1_ref, d2_ref, d3_ref, dp_ref]
    for out, start in zip(outs, starts):
        count = out.shape[0]
        out[:, k_at] = dk_buf[start : start + count, :].astype(out.dtype)
        out[:, v_at] = dv_buf[start : start + count, :].astype(out.dtype)


def attend(seen, queries, grads, cosine, sine, own, w1, w2, w3, prompt):
    rows = queries.shape[0]
    wide = own.shape[1]
    count = prompt.shape[0]
    keys = SPAN * rows + count
    head = pl.BlockSpec((rows, GROUP * HD), lambda i, s: (0, i))

    def whole(shape):
        return pl.BlockSpec(shape, lambda i, s: (0, 0))

    block = whole((rows, wide))
    return pl.pallas_call(
        attend_kernel,
        grid_spec=pltpu.PrefetchScalarGridSpec(
            num_scalar_prefetch=1,
            grid=(KVH,),
            in_specs=[head, head, whole((rows, HD)), whole((rows, HD))]
            + [block] * 4
            + [whole((count, wide))],
            out_specs=[head, head] + [block] * 4 + [whole((count, wide))],
            scratch_shapes=[pltpu.VMEM((keys, HD), bf16)] * 2 + [pltpu.VMEM((keys, HD), f32)] * 2,
        ),
        out_shape=[
            jax.ShapeDtypeStruct(queries.shape, bf16),
            jax.ShapeDtypeStruct(queries.shape, bf16),
            jax.ShapeDtypeStruct((rows, wide), f32),
            jax.ShapeDtypeStruct((rows, wide), bf16),
            jax.ShapeDtypeStruct((rows, wide), f32),
            jax.ShapeDtypeStruct((rows, wide), bf16),
            jax.ShapeDtypeStruct((count, wide), f32),
        ],
        compiler_params=pltpu.CompilerParams(vmem_limit_bytes=56 * 2**20),
        name="attend",
    )(seen, queries, grads, cosine, sine, own, w1, w2, w3, prompt)


def local(
    queries, answer_keys, answer_values, prompt_keys, prompt_values, positions, ancestry, out_grad
):
    n = lax.axis_size("ctx")
    width = answer_keys.shape[1]
    me = lax.axis_index("ctx")
    core = me % 2
    swap = [(i, i ^ 1) for i in range(n)]
    ahead = [(i, i + 2) for i in range(n - 2)]
    across = [(i, i + 1) for i in range(0, n, 2)] + [(i, i + 3) for i in range(1, n - 3, 2)]

    def back(pairs):
        return [(b, a) for a, b in pairs]

    prompt_rows = prompt_keys.shape[0]
    prompt_places = me * prompt_rows + jnp.arange(prompt_rows, dtype=jnp.int32)
    pcos, psin = angle_tables(prompt_places)
    mine = jnp.concatenate([rotate(prompt_keys, pcos, psin).astype(bf16), prompt_values], axis=1)
    chip = jnp.concatenate([mine, permute(mine, swap)], axis=0)

    cosine, sine = angle_tables(positions)
    own = jnp.concatenate([rotate(answer_keys, cosine, sine).astype(bf16), answer_values], axis=1)
    w2 = permute(own, ahead)
    w1 = permute(own, across)
    w3 = permute(w2, swap)
    rounds = [[(i, (i + 2 * k) % n) for i in range(n)] for k in range(1, n // 2)]
    prompt = jnp.concatenate([chip] + [permute(chip, pairs) for pairs in rounds], axis=0)

    table = ancestry[0]
    steps = jnp.stack([3 - 2 * core, 2 + 0 * core, 1 + 2 * core])
    match = jnp.arange(table.shape[0], dtype=jnp.int32)[None, :] == (me - steps)[:, None]
    seen = jnp.sum(jnp.where(match, table[None, :], 0), axis=1).astype(jnp.int32)

    attended, grad_queries, d0, d1, d2, d3, dp = attend(
        seen, queries, out_grad, cosine, sine, own, w1, w2, w3, prompt
    )
    r3 = permute(d3, swap)
    r1 = permute(d1, back(across))
    r2 = permute((d2 + r3.astype(f32)).astype(bf16), back(ahead))
    terms = dp.reshape(n // 2, 2 * prompt_rows, 2 * width)
    total = terms[0]
    for k, pairs in enumerate(rounds):
        total = total + permute(terms[k + 1], back(pairs))
    prompt_sum = total[:prompt_rows] + permute(total[prompt_rows:], swap)

    summed = d0 + (r1.astype(f32) + r2.astype(f32))
    grad_keys = rotate(summed[:, :width], cosine, -sine).astype(bf16)
    grad_values = summed[:, width:].astype(bf16)
    grad_prompt_keys = rotate(prompt_sum[:, :width], pcos, -psin).astype(bf16)
    grad_prompt_values = prompt_sum[:, width:].astype(bf16)
    return (attended, grad_queries, grad_keys, grad_values, grad_prompt_keys, grad_prompt_values)


def solution(mesh):
    rows = P(("groups", "ctx"), None)
    return jax.shard_map(
        local,
        mesh=mesh,
        in_specs=(rows, rows, rows, rows, rows, P(("groups", "ctx")), rows, rows),
        out_specs=(rows,) * 6,
        check_vma=False,
    )
```

```python
import jax
import jax.numpy as jnp
from jax import lax
from jax.experimental import pallas as pl
from jax.experimental.pallas import tpu as pltpu
from jax.sharding import PartitionSpec as P

QH = 20
KVH = 4
GROUP = QH // KVH
HD = 128
WIDTH = KVH * HD
SPAN = 4
SCALE = HD**-0.5
LOG2E = 1.4426950408889634
HIDDEN = -1e30

rope_base = 1000000.0

f32 = jnp.float32
bf16 = jnp.bfloat16


def permute(value, pairs):
    return lax.ppermute(value, "ctx", pairs)


def back(pairs):
    return [(b, a) for a, b in pairs]


def angle_tables(places):
    lane = jnp.arange(HD, dtype=jnp.int32)
    freqs = rope_base ** (-(2.0 * (lane % (HD // 2)).astype(f32)) / HD)
    angles = places.astype(f32)[:, None] * freqs[None, :]
    sign = jnp.where(lane < HD // 2, -1.0, 1.0).astype(f32)
    return jnp.cos(angles), jnp.sin(angles) * sign[None, :]


def dot(a, b, ca, cb):
    return lax.dot_general(a, b, (((ca,), (cb,)), ((), ())), preferred_element_type=f32)


def turn(x, cosine, sine):
    return x * cosine + pltpu.roll(x, HD // 2, 1) * sine


def attend_kernel(*refs, pieces):
    seen, q_ref, g_ref, cos_ref, sin_ref = refs[:5]
    blocks = refs[5:9]
    prompts = refs[9 : 9 + pieces]
    o_ref, dq_ref, d0_ref, d1_ref, d2_ref, d3_ref, dp_ref = refs[9 + pieces : 16 + pieces]
    k_buf, v_buf, dk_buf, dv_buf, pk_buf, pv_buf = refs[16 + pieces :]
    rows = q_ref.shape[0]
    count = prompts[0].shape[0]
    half = count // 2
    col = pl.program_id(0) * HD
    k_at = pl.ds(pl.multiple_of(col, HD), HD)
    v_at = pl.ds(pl.multiple_of(col + WIDTH, HD), HD)
    for j, part in enumerate(blocks):
        span = slice(j * rows, (j + 1) * rows)
        raw = part[:, k_at].astype(f32)
        k_buf[span, :] = turn(raw, cos_ref[span, :], sin_ref[span, :]).astype(bf16)
        v_buf[span, :] = part[:, v_at]
    for j, part in enumerate(prompts):
        span = slice(j * count, (j + 1) * count)
        pk_buf[span, :] = part[:, k_at].astype(f32)
        pv_buf[span, :] = part[:, v_at].astype(f32)
    span = slice(SPAN * rows, SPAN * rows + pieces * count)
    k_buf[span, :] = turn(pk_buf[...], cos_ref[span, :], sin_ref[span, :]).astype(bf16)
    v_buf[span, :] = pv_buf[...].astype(bf16)
    k, v = k_buf[...], v_buf[...]
    cosine, sine = cos_ref[:rows, :], sin_ref[:rows, :]
    lower = lax.broadcasted_iota(jnp.int32, (rows, rows), 1) <= lax.broadcasted_iota(
        jnp.int32, (rows, rows), 0
    )
    bias = [jnp.where(seen[i] > 0, 0.0, HIDDEN).astype(f32) for i in range(3)]
    for h in range(GROUP):
        cols = slice(h * HD, (h + 1) * HD)
        q = turn(q_ref[:, cols].astype(f32), cosine, sine).astype(bf16)
        g = g_ref[:, cols]
        s = dot(q, k, 1, 1)
        s_own = jnp.where(lower, s[:, :rows], HIDDEN)
        s_win = [s[:, rows * (i + 1) : rows * (i + 2)] for i in range(3)]
        s_pr = s[:, 4 * rows :]
        peak = jnp.maximum(
            jnp.max(s_own, axis=1, keepdims=True), jnp.max(s_pr, axis=1, keepdims=True)
        )
        for i in range(3):
            peak = jnp.maximum(peak, jnp.max(s_win[i], axis=1, keepdims=True) + bias[i])
        base = peak * (SCALE * LOG2E)
        e = (
            [jnp.exp2(s_own * (SCALE * LOG2E) - base)]
            + [jnp.exp2(s_win[i] * (SCALE * LOG2E) - (base - bias[i])) for i in range(3)]
            + [jnp.exp2(s_pr * (SCALE * LOG2E) - base)]
        )
        total = sum(jnp.sum(x, axis=1, keepdims=True) for x in e)
        w = jnp.concatenate(e, axis=1) * (1.0 / total)
        wb = w.astype(bf16)
        o = dot(wb, v, 1, 0).astype(bf16)
        o_ref[:, cols] = o
        delta = jnp.sum(o.astype(f32) * g.astype(f32), axis=1, keepdims=True)
        dw = dot(g, v, 1, 1)
        ds = (w * (dw - delta) * SCALE).astype(bf16)
        dq_ref[:, cols] = turn(dot(ds, k, 1, 0), cosine, -sine).astype(bf16)
        dk, dv = dot(ds, q, 0, 0), dot(wb, g, 0, 0)
        if h == 0:
            dk_buf[...] = dk
            dv_buf[...] = dv
        else:
            dk_buf[...] += dk
            dv_buf[...] += dv
    outs = [d0_ref, d1_ref, d2_ref, d3_ref]
    for at, buf in ((k_at, dk_buf), (v_at, dv_buf)):
        for j, out in enumerate(outs):
            out[:rows, at] = buf[j * rows : (j + 1) * rows, :].astype(out.dtype)
        for j in range(pieces):
            start = SPAN * rows + j * count
            dp_ref[j * half : (j + 1) * half, at] = buf[start : start + half, :]
            d3_ref[rows + j * half : rows + (j + 1) * half, at] = buf[
                start + half : start + count, :
            ]


def attend(seen, queries, grads, cosine, sine, blocks, prompts):
    rows = queries.shape[0]
    wide = blocks[0].shape[1]
    pieces, count = len(prompts), prompts[0].shape[0]
    keys = SPAN * rows + pieces * count
    half = pieces * count // 2
    head = pl.BlockSpec((rows, GROUP * HD), lambda i, s: (0, i))

    def whole(*shape):
        return pl.BlockSpec(shape, lambda i, s: (0, 0))

    def body(*refs):
        attend_kernel(*refs, pieces=pieces)

    outs = [(rows, f32), (rows, bf16), (rows, f32), (rows + half, f32), (half, f32)]
    return pl.pallas_call(
        body,
        grid_spec=pltpu.PrefetchScalarGridSpec(
            num_scalar_prefetch=1,
            grid=(KVH,),
            in_specs=[head, head, whole(keys, HD), whole(keys, HD)]
            + [whole(rows, wide)] * 4
            + [whole(count, wide)] * pieces,
            out_specs=[head, head] + [whole(r, wide) for r, _ in outs],
            scratch_shapes=[pltpu.VMEM((keys, HD), bf16)] * 2
            + [pltpu.VMEM((keys, HD), f32)] * 2
            + [pltpu.VMEM((pieces * count, HD), f32)] * 2,
        ),
        out_shape=[jax.ShapeDtypeStruct(queries.shape, bf16)] * 2
        + [jax.ShapeDtypeStruct((r, wide), t) for r, t in outs],
        compiler_params=pltpu.CompilerParams(vmem_limit_bytes=56 * 2**20),
        name="attend",
    )(seen, queries, grads, cosine, sine, *blocks, *prompts)


def merge_kernel(d2_ref, r3_ref, dp_ref, x2_ref, *outs):
    rows = d2_ref.shape[0]
    x2_ref[...] = (d2_ref[...] + r3_ref[:rows, :]).astype(bf16)
    for j, out in enumerate(outs):
        step = out.shape[0]
        span = slice(j * step, (j + 1) * step)
        out[...] = dp_ref[span, :] + r3_ref[rows + j * step : rows + (j + 1) * step, :]


def merge(d2, r3, dp, pieces):
    rows, wide = d2.shape
    return pl.pallas_call(
        merge_kernel,
        out_shape=[jax.ShapeDtypeStruct((rows, wide), bf16)]
        + [jax.ShapeDtypeStruct((dp.shape[0] // pieces, wide), f32)] * pieces,
        name="merge",
    )(d2, r3, dp)


def finish_kernel(*refs, pieces):
    d0_ref, r1_ref, r2_ref, cos_ref, sin_ref, pcos_ref, psin_ref = refs[:7]
    terms = refs[7 : 7 + pieces]
    gk_ref, gv_ref, gpk_ref, gpv_ref = refs[7 + pieces :]
    rows = d0_ref.shape[0]
    cosine, sine = cos_ref[:rows, :], -sin_ref[:rows, :]
    pcos, psin = pcos_ref[...], -psin_ref[...]
    for h in range(KVH):
        at = slice(h * HD, (h + 1) * HD)
        vat = slice(WIDTH + h * HD, WIDTH + (h + 1) * HD)
        for cols, out in ((at, gk_ref), (vat, gv_ref)):
            total = d0_ref[:, cols] + (r1_ref[:, cols].astype(f32) + r2_ref[:, cols].astype(f32))
            out[:, at] = (turn(total, cosine, sine) if out is gk_ref else total).astype(bf16)
        for cols, out in ((at, gpk_ref), (vat, gpv_ref)):
            total = terms[0][:, cols]
            for term in terms[1:]:
                total = total + term[:, cols]
            out[:, at] = (turn(total, pcos, psin) if out is gpk_ref else total).astype(bf16)


def finish(d0, r1, r2, cosine, sine, pcos, psin, terms):
    rows = d0.shape[0]
    few = terms[0].shape[0]
    pieces = len(terms)

    def body(*refs):
        finish_kernel(*refs, pieces=pieces)

    return pl.pallas_call(
        body,
        out_shape=[jax.ShapeDtypeStruct((r, WIDTH), bf16) for r in (rows, rows, few, few)],
        name="finish",
    )(d0, r1, r2, cosine, sine, pcos, psin, *terms)


def local(
    queries, answer_keys, answer_values, prompt_keys, prompt_values, positions, ancestry, out_grad
):
    n = lax.axis_size("ctx")
    rows = queries.shape[0]
    me = lax.axis_index("ctx")
    core = me & 1
    swap = [(i, i ^ 1) for i in range(n)]
    ahead = [(i, i + 2) for i in range(n - 2)]
    across = [(i, i + 1) for i in range(0, n, 2)] + [(i, i + 3) for i in range(1, n - 3, 2)]
    rounds = [[(i, (i + 2 * k) % n) for i in range(n)] for k in range(1, n // 2)]

    mine = jnp.concatenate([prompt_keys, prompt_values], axis=1)
    chip = jnp.concatenate([mine, permute(mine, swap)], axis=0)
    own = jnp.concatenate([answer_keys, answer_values], axis=1)
    w2 = permute(own, ahead)
    w1 = permute(own, across)
    prompts = [chip] + [permute(chip, pairs) for pairs in rounds]
    w3 = permute(w2, swap)

    few = prompt_keys.shape[0]
    table = ancestry[0]
    column = jnp.arange(table.shape[0], dtype=jnp.int32)[None, :]
    steps = jnp.arange(SPAN, dtype=jnp.int32)
    steps = jnp.where((core == 0) & (steps > 0), SPAN - steps, steps)
    first = me - steps
    seen = jnp.sum(jnp.where(column == first[:, None], table[None, :], 0), axis=1)
    apart = jnp.sum(
        jnp.where((column >= first[:, None]) & (column < me), table[None, :], 0), axis=1
    )
    places = (positions[None, :] - rows * apart[:, None]).reshape(-1)
    chips = (me // 2 - jnp.arange(n // 2, dtype=jnp.int32)) % (n // 2)
    sides = jnp.stack([core, 1 - core])
    devices = 2 * chips[:, None] + sides[None, :]
    prompt_places = (devices[:, :, None] * few + jnp.arange(few, dtype=jnp.int32)).reshape(-1)
    cosine, sine = angle_tables(jnp.concatenate([places, prompt_places]))
    pcos, psin = cosine[SPAN * rows : SPAN * rows + few], sine[SPAN * rows : SPAN * rows + few]

    attended, grad_queries, d0, d1, d2, d3, dp = attend(
        seen[1:], queries, out_grad, cosine, sine, [own, w1, w2, w3], prompts
    )
    r3 = permute(d3, swap)
    r1 = permute(d1, back(across))
    x2, *terms = merge(d2, r3, dp, n // 2)
    r2 = permute(x2, back(ahead))
    terms = [terms[0]] + [permute(t, back(pairs)) for t, pairs in zip(terms[1:], rounds)]
    grad_keys, grad_values, grad_prompt_keys, grad_prompt_values = finish(
        d0, r1, r2, cosine, sine, pcos, psin, terms
    )
    return (attended, grad_queries, grad_keys, grad_values, grad_prompt_keys, grad_prompt_values)


def solution(mesh):
    rows = P(("groups", "ctx"), None)
    return jax.shard_map(
        local,
        mesh=mesh,
        in_specs=(rows, rows, rows, rows, rows, P(("groups", "ctx")), rows, rows),
        out_specs=(rows,) * 6,
        check_vma=False,
    )
```

```python
import jax
import jax.numpy as jnp
from jax import lax
from jax.experimental import pallas as pl
from jax.experimental.pallas import tpu as pltpu
from jax.sharding import PartitionSpec as P

QH = 20
KVH = 4
GROUP = QH // KVH
HD = 128
WIDTH = KVH * HD
SPAN = 4
SCALE = HD**-0.5
LOG2E = 1.4426950408889634
HIDDEN = -1e30

rope_base = 1000000.0

f32 = jnp.float32
bf16 = jnp.bfloat16


def permute(value, pairs):
    return lax.ppermute(value, "ctx", pairs)


def back(pairs):
    return [(b, a) for a, b in pairs]


def angle_tables(places):
    lane = jnp.arange(HD, dtype=jnp.int32)
    freqs = rope_base ** (-(2.0 * (lane % (HD // 2)).astype(f32)) / HD)
    angles = places.astype(f32)[:, None] * freqs[None, :]
    sign = jnp.where(lane < HD // 2, -1.0, 1.0).astype(f32)
    return jnp.cos(angles), jnp.sin(angles) * sign[None, :]


def dot(a, b, ca, cb):
    return lax.dot_general(a, b, (((ca,), (cb,)), ((), ())), preferred_element_type=f32)


def turn(x, cosine, sine):
    return x * cosine + pltpu.roll(x, HD // 2, 1) * sine


IN_VMEM = pl.BlockSpec(memory_space=pltpu.VMEM)


def stack(a, b):
    return jnp.concatenate([a, b], axis=0)


def pack_kernel(k_ref, v_ref, pk_ref, pv_ref, own_ref, mine_ref):
    own_ref[:, :WIDTH] = k_ref[...]
    own_ref[:, WIDTH:] = v_ref[...]
    mine_ref[:, :WIDTH] = pk_ref[...]
    mine_ref[:, WIDTH:] = pv_ref[...]


def pack(keys, values, prompt_keys, prompt_values):
    return pl.pallas_call(
        pack_kernel,
        out_shape=[
            jax.ShapeDtypeStruct((keys.shape[0], 2 * WIDTH), bf16),
            jax.ShapeDtypeStruct((prompt_keys.shape[0], 2 * WIDTH), bf16),
        ],
        out_specs=[IN_VMEM, IN_VMEM],
        name="pack",
    )(keys, values, prompt_keys, prompt_values)


def attend_kernel(
    seen, q_ref, g_ref, cos_ref, sin_ref, own_ref, w1_ref, w2_ref, w3_ref, pa_ref, pb_ref,
    o_ref, dq_ref, d0_ref, d1_ref, d2_ref, d3_ref, dp_ref,
    k_buf, v_buf, dk_buf, dv_buf, p_buf,
):
    rows = q_ref.shape[0]
    half = pa_ref.shape[0]
    core = seen[3]
    col = pl.program_id(0) * HD
    k_at = pl.ds(pl.multiple_of(col, HD), HD)
    v_at = pl.ds(pl.multiple_of(col + WIDTH, HD), HD)
    for j, part in enumerate((own_ref, w1_ref, w2_ref, w3_ref)):
        span = slice(j * rows, (j + 1) * rows)
        raw = part[:, k_at].astype(f32)
        k_buf[span, :] = turn(raw, cos_ref[span, :], sin_ref[span, :]).astype(bf16)
        v_buf[span, :] = part[:, v_at]
    mine = pl.ds(pl.multiple_of(core * half, half), half)
    other = pl.ds(pl.multiple_of((1 - core) * half, half), half)
    span = slice(SPAN * rows, SPAN * rows + 2 * half)
    p_buf[mine, :] = pa_ref[:, k_at].astype(f32)
    p_buf[other, :] = pb_ref[:, k_at].astype(f32)
    k_buf[span, :] = turn(p_buf[...], cos_ref[span, :], sin_ref[span, :]).astype(bf16)
    p_buf[mine, :] = pa_ref[:, v_at].astype(f32)
    p_buf[other, :] = pb_ref[:, v_at].astype(f32)
    v_buf[span, :] = p_buf[...].astype(bf16)
    k, v = k_buf[...], v_buf[...]
    cosine, sine = cos_ref[:rows, :], sin_ref[:rows, :]
    lower = lax.broadcasted_iota(jnp.int32, (rows, rows), 1) <= lax.broadcasted_iota(
        jnp.int32, (rows, rows), 0
    )
    bias = [jnp.where(seen[i] > 0, 0.0, HIDDEN).astype(f32) for i in range(3)]

    def cols(h):
        return slice(h * HD, (h + 1) * HD)

    def open_head(h):
        q = turn(q_ref[:, cols(h)].astype(f32), cosine, sine).astype(bf16)
        g = g_ref[:, cols(h)]
        return q, g, dot(q, k, 1, 1), dot(g, v, 1, 1)

    def weigh(s):
        s_own = jnp.where(lower, s[:, :rows], HIDDEN)
        s_win = [s[:, rows * (i + 1) : rows * (i + 2)] for i in range(3)]
        s_pr = s[:, SPAN * rows :]
        peak = jnp.maximum(
            jnp.max(s_own, axis=1, keepdims=True), jnp.max(s_pr, axis=1, keepdims=True)
        )
        for i in range(3):
            peak = jnp.maximum(peak, jnp.max(s_win[i], axis=1, keepdims=True) + bias[i])
        base = peak * (SCALE * LOG2E)
        e = (
            [jnp.exp2(s_own * (SCALE * LOG2E) - base)]
            + [jnp.exp2(s_win[i] * (SCALE * LOG2E) - (base - bias[i])) for i in range(3)]
            + [jnp.exp2(s_pr * (SCALE * LOG2E) - base)]
        )
        total = sum(jnp.sum(x, axis=1, keepdims=True) for x in e)
        return jnp.concatenate(e, axis=1) * (1.0 / total)

    def close_head(h, ds, wb, q, g):
        dq_ref[:, cols(h)] = turn(dot(ds, k, 1, 0), cosine, -sine).astype(bf16)
        dk, dv = dot(ds, q, 0, 0), dot(wb, g, 0, 0)
        if h == 0:
            dk_buf[...] = dk
            dv_buf[...] = dv
        else:
            dk_buf[...] += dk
            dv_buf[...] += dv

    ahead, behind = open_head(0), None
    for h in range(GROUP):
        q, g, s, dw = ahead
        if h + 1 < GROUP:
            ahead = open_head(h + 1)
        if behind is not None:
            close_head(*behind)
        w = weigh(s)
        wb = w.astype(bf16)
        o = dot(wb, v, 1, 0).astype(bf16)
        o_ref[:, cols(h)] = o
        delta = jnp.sum(o.astype(f32) * g.astype(f32), axis=1, keepdims=True)
        behind = (h, (w * (dw - delta) * SCALE).astype(bf16), wb, q, g)
    close_head(*behind)

    start = SPAN * rows
    for at, buf in ((k_at, dk_buf), (v_at, dv_buf)):
        for j, out in enumerate((d0_ref, d1_ref, d2_ref, d3_ref)):
            out[:rows, at] = buf[j * rows : (j + 1) * rows, :].astype(out.dtype)
        dp_ref[:, at] = buf[pl.ds(pl.multiple_of(start + core * half, 8), half), :]
        d3_ref[rows:, at] = buf[pl.ds(pl.multiple_of(start + (1 - core) * half, 8), half), :]


def attend(seen, queries, grads, cosine, sine, blocks, prompts):
    rows = queries.shape[0]
    wide = blocks[0].shape[1]
    half = prompts[0].shape[0]
    keys = SPAN * rows + 2 * half
    head = pl.BlockSpec((rows, GROUP * HD), lambda i, s: (0, i))
    outs = [(rows, f32), (rows, bf16), (rows, f32), (rows + half, f32), (half, f32)]
    return pl.pallas_call(
        attend_kernel,
        grid_spec=pltpu.PrefetchScalarGridSpec(
            num_scalar_prefetch=1,
            grid=(KVH,),
            in_specs=[head, head] + [IN_VMEM] * 8,
            out_specs=[head, head] + [IN_VMEM] * 5,
            scratch_shapes=[pltpu.VMEM((keys, HD), bf16)] * 2
            + [pltpu.VMEM((keys, HD), f32)] * 2
            + [pltpu.VMEM((2 * half, HD), f32)],
        ),
        out_shape=[jax.ShapeDtypeStruct(queries.shape, bf16)] * 2
        + [jax.ShapeDtypeStruct((r, wide), t) for r, t in outs],
        compiler_params=pltpu.CompilerParams(vmem_limit_bytes=40 * 2**20),
        name="attend",
    )(seen, queries, grads, cosine, sine, *blocks, *prompts)


def merge_kernel(d2_ref, r3_ref, dp_ref, x2_ref, *outs):
    rows = d2_ref.shape[0]
    x2_ref[...] = (d2_ref[...] + r3_ref[:rows, :]).astype(bf16)
    for j, out in enumerate(outs):
        step = out.shape[0]
        span = slice(j * step, (j + 1) * step)
        out[...] = dp_ref[span, :] + r3_ref[rows + j * step : rows + (j + 1) * step, :]


def merge(d2, r3, dp, pieces):
    rows, wide = d2.shape
    return pl.pallas_call(
        merge_kernel,
        in_specs=[IN_VMEM] * 3,
        out_specs=[IN_VMEM] * (1 + pieces),
        out_shape=[jax.ShapeDtypeStruct((rows, wide), bf16)]
        + [jax.ShapeDtypeStruct((dp.shape[0] // pieces, wide), f32)] * pieces,
        name="merge",
    )(d2, r3, dp)


def tally_kernel(core_ref, *refs):
    terms, keep_ref, send_ref = refs[:-2], refs[-2], refs[-1]
    few = keep_ref.shape[0]
    total = terms[0][...]
    for term in terms[1:]:
        total = total + term[...]
    first = core_ref[0] == 0
    keep_ref[...] = jnp.where(first, total[:few], total[few:])
    send_ref[...] = jnp.where(first, total[few:], total[:few])


def tally(core, terms):
    few, wide = terms[0].shape
    return pl.pallas_call(
        tally_kernel,
        in_specs=[pl.BlockSpec(memory_space=pltpu.SMEM)] + [IN_VMEM] * len(terms),
        out_specs=[IN_VMEM] * 2,
        out_shape=[jax.ShapeDtypeStruct((few // 2, wide), f32)] * 2,
        name="tally",
    )(core, *terms)


def finish_kernel(
    d0_ref, r1_ref, r2_ref, cos_ref, sin_ref, pcos_ref, psin_ref, keep_ref, got_ref,
    gk_ref, gv_ref, gpk_ref, gpv_ref,
):
    rows = d0_ref.shape[0]
    cosine, sine = cos_ref[:rows, :], -sin_ref[:rows, :]
    pcos, psin = pcos_ref[...], -psin_ref[...]
    for h in range(KVH):
        at = slice(h * HD, (h + 1) * HD)
        vat = slice(WIDTH + h * HD, WIDTH + (h + 1) * HD)
        for cols, out in ((at, gk_ref), (vat, gv_ref)):
            total = d0_ref[:, cols] + (r1_ref[:, cols].astype(f32) + r2_ref[:, cols].astype(f32))
            out[:, at] = (turn(total, cosine, sine) if out is gk_ref else total).astype(bf16)
        for cols, out in ((at, gpk_ref), (vat, gpv_ref)):
            total = keep_ref[:, cols] + got_ref[:, cols]
            out[:, at] = (turn(total, pcos, psin) if out is gpk_ref else total).astype(bf16)


def finish(d0, r1, r2, cosine, sine, pcos, psin, keep, got):
    rows, few = d0.shape[0], keep.shape[0]
    return pl.pallas_call(
        finish_kernel,
        in_specs=[IN_VMEM] * 9,
        out_shape=[jax.ShapeDtypeStruct((r, WIDTH), bf16) for r in (rows, rows, few, few)],
        name="finish",
    )(d0, r1, r2, cosine, sine, pcos, psin, keep, got)


def local(
    queries, answer_keys, answer_values, prompt_keys, prompt_values, positions, ancestry, out_grad
):
    n = lax.axis_size("ctx")
    chips = n // 2
    rows = queries.shape[0]
    few = prompt_keys.shape[0]
    me = lax.axis_index("ctx")
    core = me & 1
    swap = [(i, i ^ 1) for i in range(n)]
    ahead = [(i, i + 2) for i in range(n - 2)]
    across = [(i, i + 1) for i in range(0, n, 2)] + [(i, i + 3) for i in range(1, n - 3, 2)]
    reach = [[j, (j + chips // 2) % chips] for j in range(1, chips // 2 + 1)]
    rounds = [[(i, (i + 2 * k[i % 2]) % n) for i in range(n)] for k in reach]

    own, mine = pack(answer_keys, answer_values, prompt_keys, prompt_values)
    w2 = permute(own, ahead)
    w1 = permute(own, across)
    theirs = permute(mine, swap)
    chip = jnp.where(core == 0, stack(mine, theirs), stack(theirs, mine))
    near = jnp.concatenate([permute(chip, pairs) for pairs in rounds], axis=0)
    w3 = permute(w2, swap)
    far = permute(near, swap)

    table = ancestry[0]
    column = jnp.arange(table.shape[0], dtype=jnp.int32)[None, :]
    steps = jnp.arange(SPAN, dtype=jnp.int32)
    steps = jnp.where((core == 0) & (steps > 0), SPAN - steps, steps)
    first = me - steps
    seen = jnp.sum(jnp.where(column == first[:, None], table[None, :], 0), axis=1)
    apart = jnp.sum(
        jnp.where((column >= first[:, None]) & (column < me), table[None, :], 0), axis=1
    )
    places = (positions[None, :] - rows * apart[:, None]).reshape(-1)
    away = jnp.array([k[0] for k in reach] + [k[1] for k in reach], dtype=jnp.int32)
    homes = (me // 2 - away + chips) % chips
    prompt_places = homes[:, None] * (2 * few) + jnp.arange(2 * few, dtype=jnp.int32)
    cosine, sine = angle_tables(jnp.concatenate([places, prompt_places.reshape(-1)]))
    pcos, psin = angle_tables(me * few + jnp.arange(few, dtype=jnp.int32))
    scalars = jnp.concatenate([seen[1:], core[None]]).astype(jnp.int32)

    attended, grad_queries, d0, d1, d2, d3, dp = attend(
        scalars, queries, out_grad, cosine, sine, [own, w1, w2, w3], [near, far]
    )
    r3 = permute(d3, swap)
    r1 = permute(d1, back(across))
    x2, *terms = merge(d2, r3, dp, chips // 2)
    r2 = permute(x2, back(ahead))
    keep, send = tally(
        core[None].astype(jnp.int32), [permute(t, back(p)) for t, p in zip(terms, rounds)]
    )
    got = permute(send, swap)
    grad_keys, grad_values, grad_prompt_keys, grad_prompt_values = finish(
        d0, r1, r2, cosine, sine, pcos, psin, keep, got
    )
    return (attended, grad_queries, grad_keys, grad_values, grad_prompt_keys, grad_prompt_values)


def solution(mesh):
    rows = P(("groups", "ctx"), None)
    return jax.shard_map(
        local,
        mesh=mesh,
        in_specs=(rows, rows, rows, rows, rows, P(("groups", "ctx")), rows, rows),
        out_specs=(rows,) * 6,
        check_vma=False,
    )
```

```python
import jax
import jax.numpy as jnp
from jax import lax
from jax.experimental import pallas as pl
from jax.experimental.pallas import tpu as pltpu
from jax.sharding import PartitionSpec as P

QH = 20
KVH = 4
GROUP = QH // KVH
HD = 128
WIDTH = KVH * HD
SPAN = 4
SCALE = HD**-0.5
LOG2E = 1.4426950408889634
HIDDEN = -1e30

rope_base = 1000000.0

f32 = jnp.float32
bf16 = jnp.bfloat16


def permute(value, pairs):
    return lax.ppermute(value, "ctx", pairs)


def back(pairs):
    return [(b, a) for a, b in pairs]


def angle_tables(places):
    lane = jnp.arange(HD, dtype=jnp.int32)
    freqs = rope_base ** (-(2.0 * (lane % (HD // 2)).astype(f32)) / HD)
    angles = places.astype(f32)[:, None] * freqs[None, :]
    sign = jnp.where(lane < HD // 2, -1.0, 1.0).astype(f32)
    return jnp.cos(angles), jnp.sin(angles) * sign[None, :]


def dot(a, b, ca, cb):
    return lax.dot_general(a, b, (((ca,), (cb,)), ((), ())), preferred_element_type=f32)


def turn(x, cosine, sine):
    return x * cosine + pltpu.roll(x, HD // 2, 1) * sine


IN_VMEM = pl.BlockSpec(memory_space=pltpu.VMEM)


def pack_kernel(k_ref, v_ref, pk_ref, pv_ref, own_ref, mine_ref):
    rows, few = k_ref.shape[0], pk_ref.shape[0]
    own_ref[:rows, :WIDTH] = k_ref[...]
    own_ref[:rows, WIDTH:] = v_ref[...]
    mine_ref[:, :WIDTH] = pk_ref[...]
    mine_ref[:, WIDTH:] = pv_ref[...]
    twice = jnp.concatenate([mine_ref[...].astype(f32)] * 2, axis=0)
    own_ref[rows:, :] = twice.astype(bf16)


def pack(keys, values, prompt_keys, prompt_values):
    return pl.pallas_call(
        pack_kernel,
        out_shape=[
            jax.ShapeDtypeStruct((keys.shape[0] + 2 * prompt_keys.shape[0], 2 * WIDTH), bf16),
            jax.ShapeDtypeStruct((prompt_keys.shape[0], 2 * WIDTH), bf16),
        ],
        out_specs=[IN_VMEM, IN_VMEM],
        compiler_params=pltpu.CompilerParams(vmem_limit_bytes=6 * 2**20),
        name="pack",
    )(keys, values, prompt_keys, prompt_values)


def attend_kernel(
    seen, q_ref, g_ref, cos_ref, sin_ref, own_ref, w1_ref, w2_ref, w3_ref,
    mine_ref, theirs_ref, near_ref, far_ref,
    o_ref, dq_ref, d0_ref, d1_ref, d2_ref, d3_ref, dp_ref,
    k_buf, v_buf, dk_buf, dv_buf, p_buf,
):
    rows = q_ref.shape[0]
    few, half = mine_ref.shape[0], near_ref.shape[0]
    col = pl.program_id(0) * HD
    k_at = pl.ds(pl.multiple_of(col, HD), HD)
    v_at = pl.ds(pl.multiple_of(col + WIDTH, HD), HD)
    for j, part in enumerate((own_ref, w1_ref, w2_ref, w3_ref)):
        span = slice(j * rows, (j + 1) * rows)
        raw = part[:rows, k_at].astype(f32)
        k_buf[span, :] = turn(raw, cos_ref[span, :], sin_ref[span, :]).astype(bf16)
        v_buf[span, :] = part[:rows, v_at]
    span = slice(SPAN * rows, SPAN * rows + 4 * few + 2 * half)

    def gather(at):
        p_buf[:few, :] = mine_ref[:, at].astype(f32)
        p_buf[few : 2 * few, :] = theirs_ref[:, at].astype(f32)
        p_buf[2 * few : 3 * few, :] = w2_ref[rows:, at].astype(f32)[:few]
        p_buf[3 * few : 4 * few, :] = w3_ref[rows:, at].astype(f32)[:few]
        p_buf[4 * few : 4 * few + half, :] = near_ref[:, at].astype(f32)
        p_buf[4 * few + half :, :] = far_ref[:, at].astype(f32)
        return p_buf[...]

    k_buf[span, :] = turn(gather(k_at), cos_ref[span, :], sin_ref[span, :]).astype(bf16)
    v_buf[span, :] = gather(v_at).astype(bf16)
    k, v = k_buf[...], v_buf[...]
    cosine, sine = cos_ref[:rows, :], sin_ref[:rows, :]
    lower = lax.broadcasted_iota(jnp.int32, (rows, rows), 1) <= lax.broadcasted_iota(
        jnp.int32, (rows, rows), 0
    )
    bias = [jnp.where(seen[i] > 0, 0.0, HIDDEN).astype(f32) for i in range(3)]

    def cols(h):
        return slice(h * HD, (h + 1) * HD)

    def open_head(h):
        q = turn(q_ref[:, cols(h)].astype(f32), cosine, sine).astype(bf16)
        g = g_ref[:, cols(h)]
        return q, g, dot(q, k, 1, 1), dot(g, v, 1, 1)

    def weigh(s):
        s_own = jnp.where(lower, s[:, :rows], HIDDEN)
        s_win = [s[:, rows * (i + 1) : rows * (i + 2)] for i in range(3)]
        s_pr = s[:, SPAN * rows :]
        peak = jnp.maximum(
            jnp.max(s_own, axis=1, keepdims=True), jnp.max(s_pr, axis=1, keepdims=True)
        )
        for i in range(3):
            peak = jnp.maximum(peak, jnp.max(s_win[i], axis=1, keepdims=True) + bias[i])
        base = peak * (SCALE * LOG2E)
        e = (
            [jnp.exp2(s_own * (SCALE * LOG2E) - base)]
            + [jnp.exp2(s_win[i] * (SCALE * LOG2E) - (base - bias[i])) for i in range(3)]
            + [jnp.exp2(s_pr * (SCALE * LOG2E) - base)]
        )
        total = sum(jnp.sum(x, axis=1, keepdims=True) for x in e)
        return jnp.concatenate(e, axis=1) * (1.0 / total)

    def close_head(h, ds, wb, q, g):
        dq_ref[:, cols(h)] = turn(dot(ds, k, 1, 0), cosine, -sine).astype(bf16)
        dk, dv = dot(ds, q, 0, 0), dot(wb, g, 0, 0)
        if h == 0:
            dk_buf[...] = dk
            dv_buf[...] = dv
        else:
            dk_buf[...] += dk
            dv_buf[...] += dv

    ahead, behind = open_head(0), None
    for h in range(GROUP):
        q, g, s, dw = ahead
        if h + 1 < GROUP:
            ahead = open_head(h + 1)
        if behind is not None:
            close_head(*behind)
        w = weigh(s)
        wb = w.astype(bf16)
        o = dot(wb, v, 1, 0).astype(bf16)
        o_ref[:, cols(h)] = o
        delta = jnp.sum(o.astype(f32) * g.astype(f32), axis=1, keepdims=True)
        behind = (h, (w * (dw - delta) * SCALE).astype(bf16), wb, q, g)
    close_head(*behind)

    start = SPAN * rows
    for at, buf in ((k_at, dk_buf), (v_at, dv_buf)):
        for j, out in enumerate((d0_ref, d1_ref, d2_ref, d3_ref)):
            out[:rows, at] = buf[j * rows : (j + 1) * rows, :].astype(out.dtype)
        for j in range(2):
            mid = start + 2 * few * j
            dp_ref[j * few : (j + 1) * few, at] = buf[mid : mid + few, :]
            d3_ref[rows + j * few : rows + (j + 1) * few, at] = buf[mid + few : mid + 2 * few, :]
        mid = start + 4 * few
        dp_ref[2 * few :, at] = buf[mid : mid + half, :]
        d3_ref[rows + 2 * few :, at] = buf[mid + half :, :]


def attend(seen, queries, grads, cosine, sine, blocks, prompts):
    rows = queries.shape[0]
    wide = blocks[0].shape[1]
    few, half = prompts[0].shape[0], prompts[2].shape[0]
    keys = SPAN * rows + 4 * few + 2 * half
    part = half + 2 * few
    head = pl.BlockSpec((rows, GROUP * HD), lambda i, s: (0, i))
    outs = [(rows, f32), (rows, bf16), (rows, f32), (rows + part, f32), (part, f32)]
    return pl.pallas_call(
        attend_kernel,
        grid_spec=pltpu.PrefetchScalarGridSpec(
            num_scalar_prefetch=1,
            grid=(KVH,),
            in_specs=[head, head] + [IN_VMEM] * 10,
            out_specs=[head, head] + [IN_VMEM] * 5,
            scratch_shapes=[pltpu.VMEM((keys, HD), bf16)] * 2
            + [pltpu.VMEM((keys, HD), f32)] * 2
            + [pltpu.VMEM((2 * part, HD), f32)],
        ),
        out_shape=[jax.ShapeDtypeStruct(queries.shape, bf16)] * 2
        + [jax.ShapeDtypeStruct((r, wide), t) for r, t in outs],
        compiler_params=pltpu.CompilerParams(vmem_limit_bytes=40 * 2**20),
        name="attend",
    )(seen, queries, grads, cosine, sine, *blocks, *prompts)


def merge_kernel(d2_ref, r3_ref, dp_ref, x2_ref, keep_ref, *outs):
    rows, few = d2_ref.shape[0], keep_ref.shape[0]
    x2_ref[:rows, :] = (d2_ref[...] + r3_ref[:rows, :]).astype(bf16)
    keep_ref[...] = dp_ref[:few, :] + r3_ref[rows : rows + few, :]
    near = dp_ref[few : 2 * few, :] + r3_ref[rows + few : rows + 2 * few, :]
    high = near.astype(bf16).astype(f32)
    x2_ref[rows:, :] = jnp.concatenate([high, near - high], axis=0).astype(bf16)
    for j, out in enumerate(outs):
        step = out.shape[0]
        at = 2 * few + j * step
        out[...] = dp_ref[at : at + step, :] + r3_ref[rows + at : rows + at + step, :]


def merge(d2, r3, dp, few, pieces):
    rows, wide = d2.shape
    return pl.pallas_call(
        merge_kernel,
        in_specs=[IN_VMEM] * 3,
        out_specs=[IN_VMEM] * (2 + pieces),
        out_shape=[
            jax.ShapeDtypeStruct((rows + 2 * few, wide), bf16),
            jax.ShapeDtypeStruct((few, wide), f32),
        ]
        + [jax.ShapeDtypeStruct((2 * few, wide), f32)] * pieces,
        compiler_params=pltpu.CompilerParams(vmem_limit_bytes=6 * 2**20),
        name="merge",
    )(d2, r3, dp)


def tally_kernel(*refs):
    terms, keep_ref, send_ref = refs[:-2], refs[-2], refs[-1]
    few = keep_ref.shape[0]
    total = terms[0][...]
    for term in terms[1:]:
        total = total + term[...]
    keep_ref[...] = total[:few]
    send_ref[...] = total[few:]


def tally(terms):
    few, wide = terms[0].shape
    return pl.pallas_call(
        tally_kernel,
        in_specs=[IN_VMEM] * len(terms),
        out_specs=[IN_VMEM] * 2,
        out_shape=[jax.ShapeDtypeStruct((few // 2, wide), f32)] * 2,
        compiler_params=pltpu.CompilerParams(vmem_limit_bytes=2 * 2**20),
        name="tally",
    )(*terms)


def finish_kernel(
    d0_ref, r1_ref, r2_ref, cos_ref, sin_ref, keep_ref, sum_ref, got_ref,
    gk_ref, gv_ref, gpk_ref, gpv_ref,
):
    rows = d0_ref.shape[0]
    cosine, sine = cos_ref[:rows, :], -sin_ref[:rows, :]
    few = keep_ref.shape[0]
    mine = slice(SPAN * rows, SPAN * rows + 2 * few)
    pcos, psin = cos_ref[mine, :][:few], -sin_ref[mine, :][:few]
    for h in range(KVH):
        at = slice(h * HD, (h + 1) * HD)
        vat = slice(WIDTH + h * HD, WIDTH + (h + 1) * HD)
        for cols, out in ((at, gk_ref), (vat, gv_ref)):
            total = d0_ref[:, cols] + (r1_ref[:, cols].astype(f32) + r2_ref[:rows, cols].astype(f32))
            out[:, at] = (turn(total, cosine, sine) if out is gk_ref else total).astype(bf16)
        for cols, out in ((at, gpk_ref), (vat, gpv_ref)):
            pair = r2_ref[rows:, cols].astype(f32)
            total = keep_ref[:, cols] + (pair[:few] + pair[few:])
            total = total + (sum_ref[:, cols] + got_ref[:, cols])
            out[:, at] = (turn(total, pcos, psin) if out is gpk_ref else total).astype(bf16)


def finish(d0, r1, r2, cosine, sine, keep, tallied, got):
    rows, few = d0.shape[0], keep.shape[0]
    return pl.pallas_call(
        finish_kernel,
        in_specs=[IN_VMEM] * 8,
        out_shape=[jax.ShapeDtypeStruct((r, WIDTH), bf16) for r in (rows, rows, few, few)],
        compiler_params=pltpu.CompilerParams(vmem_limit_bytes=6 * 2**20),
        name="finish",
    )(d0, r1, r2, cosine, sine, keep, tallied, got)


def local(
    queries, answer_keys, answer_values, prompt_keys, prompt_values, positions, ancestry, out_grad
):
    n = lax.axis_size("ctx")
    chips = n // 2
    rows = queries.shape[0]
    few = prompt_keys.shape[0]
    me = lax.axis_index("ctx")
    core = me & 1
    swap = [(i, i ^ 1) for i in range(n)]
    ahead = [(i, (i + 2) % n) for i in range(n)]
    across = [(i, i + 1) for i in range(0, n, 2)] + [(i, i + 3) for i in range(1, n - 3, 2)]
    turns = chips // 2 - 1
    reach = [(1 + j, 1 + j + turns) for j in range(1, turns + 1)]
    rounds = [[(i, (i + 2 * k[i % 2]) % n) for i in range(n)] for k in reach]

    own, mine = pack(answer_keys, answer_values, prompt_keys, prompt_values)
    w2 = permute(own, ahead)
    w1 = permute(own, across)
    theirs = permute(mine, swap)
    chip = jnp.concatenate([mine, theirs], axis=0)
    near = jnp.concatenate([permute(chip, pairs) for pairs in rounds], axis=0)
    w3 = permute(w2, swap)
    far = permute(near, swap)

    table = ancestry[0]
    column = jnp.arange(table.shape[0], dtype=jnp.int32)[None, :]
    steps = jnp.arange(SPAN, dtype=jnp.int32)
    steps = jnp.where((core == 0) & (steps > 0), SPAN - steps, steps)
    first = me - steps
    seen = jnp.sum(jnp.where(column == first[:, None], table[None, :], 0), axis=1)
    apart = jnp.sum(
        jnp.where((column >= first[:, None]) & (column < me), table[None, :], 0), axis=1
    )
    places = (positions[None, :] - rows * apart[:, None]).reshape(-1)
    low = jnp.array([k[0] for k in reach], dtype=jnp.int32)
    high = jnp.array([k[1] for k in reach], dtype=jnp.int32)
    away = jnp.concatenate(
        [jnp.array([0, 1], jnp.int32), jnp.where(core == 0, low, high), jnp.where(core == 0, high, low)]
    )
    first_core = jnp.concatenate([jnp.full((2 + turns,), core), jnp.full((turns,), 1 - core)])
    homes = 2 * ((me // 2 - away + chips) % chips)
    homes = jnp.stack([homes + first_core, homes + 1 - first_core], axis=1)
    prompt_places = homes[:, :, None] * few + jnp.arange(few, dtype=jnp.int32)
    cosine, sine = angle_tables(jnp.concatenate([places, prompt_places.reshape(-1)]))

    attended, grad_queries, d0, d1, d2, d3, dp = attend(
        seen[1:], queries, out_grad, cosine, sine, [own, w1, w2, w3], [mine, theirs, near, far]
    )
    r3 = permute(d3, swap)
    r1 = permute(d1, back(across))
    x2, keep, *terms = merge(d2, r3, dp, few, turns)
    r2 = permute(x2, back(ahead))
    tallied, send = tally([permute(t, back(p)) for t, p in zip(terms, rounds)])
    got = permute(send, swap)
    grad_keys, grad_values, grad_prompt_keys, grad_prompt_values = finish(
        d0, r1, r2, cosine, sine, keep, tallied, got
    )
    return (attended, grad_queries, grad_keys, grad_values, grad_prompt_keys, grad_prompt_values)


def solution(mesh):
    rows = P(("groups", "ctx"), None)
    return jax.shard_map(
        local,
        mesh=mesh,
        in_specs=(rows, rows, rows, rows, rows, P(("groups", "ctx")), rows, rows),
        out_specs=(rows,) * 6,
        check_vma=False,
    )
```

```python
import jax
import jax.numpy as jnp
from jax import lax
from jax.experimental import pallas as pl
from jax.experimental.pallas import tpu as pltpu
from jax.sharding import PartitionSpec as P

QH = 20
KVH = 4
GROUP = QH // KVH
HD = 128
WIDTH = KVH * HD
SPAN = 4
SCALE = HD**-0.5
LOG2E = 1.4426950408889634
HIDDEN = -1e30

rope_base = 1000000.0

f32 = jnp.float32
bf16 = jnp.bfloat16


def in_hbm(value):
    return pltpu.with_memory_space_constraint(value, pltpu.HBM)


def permute(value, pairs):
    return lax.ppermute(value, "ctx", pairs)


def back(pairs):
    return [(b, a) for a, b in pairs]


def angle_tables(places):
    lane = jnp.arange(HD, dtype=jnp.int32)
    freqs = rope_base ** (-(2.0 * (lane % (HD // 2)).astype(f32)) / HD)
    angles = places.astype(f32)[:, None] * freqs[None, :]
    sign = jnp.where(lane < HD // 2, -1.0, 1.0).astype(f32)
    return jnp.cos(angles), jnp.sin(angles) * sign[None, :]


def dot(a, b, ca, cb):
    return lax.dot_general(a, b, (((ca,), (cb,)), ((), ())), preferred_element_type=f32)


def turn(x, cosine, sine):
    return x * cosine + pltpu.roll(x, HD // 2, 1) * sine


IN_VMEM = pl.BlockSpec(memory_space=pltpu.VMEM)
IN_HBM = pl.BlockSpec(memory_space=pltpu.HBM)


def pack_kernel(k_ref, v_ref, pk_ref, pv_ref, own_ref, mine_ref, sems):
    rows = k_ref.shape[0]
    copies = [
        pltpu.make_async_copy(src, dst, sems.at[i])
        for i, (src, dst) in enumerate(
            (
                (pk_ref, mine_ref.at[:, :WIDTH]),
                (pv_ref, mine_ref.at[:, WIDTH:]),
                (k_ref, own_ref.at[:rows, :WIDTH]),
                (v_ref, own_ref.at[:rows, WIDTH:]),
            )
        )
    ]
    for copy in copies:
        copy.start()
    copies[0].wait()
    copies[1].wait()
    twice = jnp.concatenate([mine_ref[...].astype(f32)] * 2, axis=0)
    own_ref[rows:, :] = twice.astype(bf16)
    copies[2].wait()
    copies[3].wait()


def pack(keys, values, prompt_keys, prompt_values):
    rows = keys.shape[0] + 2 * prompt_keys.shape[0]
    return pl.pallas_call(
        pack_kernel,
        in_specs=[IN_HBM] * 4,
        out_shape=[
            jax.ShapeDtypeStruct((rows, 2 * WIDTH), bf16),
            jax.ShapeDtypeStruct((prompt_keys.shape[0], 2 * WIDTH), bf16),
        ],
        out_specs=[IN_VMEM, IN_VMEM],
        scratch_shapes=[pltpu.SemaphoreType.DMA((4,))],
        compiler_params=pltpu.CompilerParams(vmem_limit_bytes=4 * 2**20),
        name="pack",
    )(*(in_hbm(x) for x in (keys, values, prompt_keys, prompt_values)))


def attend_kernel(
    seen, q_ref, g_ref, cos_ref, sin_ref, own_ref, w1_ref, w2_ref, w3_ref,
    mine_ref, theirs_ref, near_ref, far_ref,
    o_ref, dq_ref, d0_ref, d1_ref, d2_ref, d3_ref, dp_ref,
    k_buf, v_buf, dk_buf, dv_buf, p_buf,
):
    rows = q_ref.shape[0]
    few, half = mine_ref.shape[0], near_ref.shape[0]
    col = pl.program_id(0) * HD
    k_at = pl.ds(pl.multiple_of(col, HD), HD)
    v_at = pl.ds(pl.multiple_of(col + WIDTH, HD), HD)
    for j, part in enumerate((own_ref, w1_ref, w2_ref, w3_ref)):
        span = slice(j * rows, (j + 1) * rows)
        raw = part[:rows, k_at].astype(f32)
        k_buf[span, :] = turn(raw, cos_ref[span, :], sin_ref[span, :]).astype(bf16)
        v_buf[span, :] = part[:rows, v_at]
    span = slice(SPAN * rows, SPAN * rows + 4 * few + 2 * half)

    def gather(at):
        p_buf[:few, :] = mine_ref[:, at].astype(f32)
        p_buf[few : 2 * few, :] = theirs_ref[:, at].astype(f32)
        p_buf[2 * few : 3 * few, :] = w2_ref[rows:, at].astype(f32)[:few]
        p_buf[3 * few : 4 * few, :] = w3_ref[rows:, at].astype(f32)[:few]
        p_buf[4 * few : 4 * few + half, :] = near_ref[:, at].astype(f32)
        p_buf[4 * few + half :, :] = far_ref[:, at].astype(f32)
        return p_buf[...]

    k_buf[span, :] = turn(gather(k_at), cos_ref[span, :], sin_ref[span, :]).astype(bf16)
    v_buf[span, :] = gather(v_at).astype(bf16)
    k, v = k_buf[...], v_buf[...]
    cosine, sine = cos_ref[:rows, :], sin_ref[:rows, :]
    lower = lax.broadcasted_iota(jnp.int32, (rows, rows), 1) <= lax.broadcasted_iota(
        jnp.int32, (rows, rows), 0
    )
    bias = [jnp.where(seen[i] > 0, 0.0, HIDDEN).astype(f32) for i in range(3)]

    def cols(h):
        return slice(h * HD, (h + 1) * HD)

    def open_head(h):
        q = turn(q_ref[:, cols(h)].astype(f32), cosine, sine).astype(bf16)
        g = g_ref[:, cols(h)]
        return q, g, dot(q, k, 1, 1), dot(g, v, 1, 1)

    def weigh(s):
        s_own = jnp.where(lower, s[:, :rows], HIDDEN)
        s_win = [s[:, rows * (i + 1) : rows * (i + 2)] for i in range(3)]
        s_pr = s[:, SPAN * rows :]
        peak = jnp.maximum(
            jnp.max(s_own, axis=1, keepdims=True), jnp.max(s_pr, axis=1, keepdims=True)
        )
        for i in range(3):
            peak = jnp.maximum(peak, jnp.max(s_win[i], axis=1, keepdims=True) + bias[i])
        base = peak * (SCALE * LOG2E)
        e = (
            [jnp.exp2(s_own * (SCALE * LOG2E) - base)]
            + [jnp.exp2(s_win[i] * (SCALE * LOG2E) - (base - bias[i])) for i in range(3)]
            + [jnp.exp2(s_pr * (SCALE * LOG2E) - base)]
        )
        total = sum(jnp.sum(x, axis=1, keepdims=True) for x in e)
        return jnp.concatenate(e, axis=1) * (1.0 / total)

    def close_head(h, ds, wb, q, g):
        dq_ref[:, cols(h)] = turn(dot(ds, k, 1, 0), cosine, -sine).astype(bf16)
        dk, dv = dot(ds, q, 0, 0), dot(wb, g, 0, 0)
        if h == 0:
            dk_buf[...] = dk
            dv_buf[...] = dv
        else:
            dk_buf[...] += dk
            dv_buf[...] += dv

    ahead, behind = open_head(0), None
    for h in range(GROUP):
        q, g, s, dw = ahead
        if h + 1 < GROUP:
            ahead = open_head(h + 1)
        if behind is not None:
            close_head(*behind)
        w = weigh(s)
        wb = w.astype(bf16)
        o = dot(wb, v, 1, 0).astype(bf16)
        o_ref[:, cols(h)] = o
        delta = jnp.sum(o.astype(f32) * g.astype(f32), axis=1, keepdims=True)
        behind = (h, (w * (dw - delta) * SCALE).astype(bf16), wb, q, g)
    close_head(*behind)

    start = SPAN * rows
    for at, buf in ((k_at, dk_buf), (v_at, dv_buf)):
        for j, out in enumerate((d0_ref, d1_ref, d2_ref, d3_ref)):
            out[:rows, at] = buf[j * rows : (j + 1) * rows, :].astype(out.dtype)
        for j in range(2):
            mid = start + 2 * few * j
            dp_ref[j * few : (j + 1) * few, at] = buf[mid : mid + few, :]
            d3_ref[rows + j * few : rows + (j + 1) * few, at] = buf[mid + few : mid + 2 * few, :]
        mid = start + 4 * few
        dp_ref[2 * few :, at] = buf[mid : mid + half, :]
        d3_ref[rows + 2 * few :, at] = buf[mid + half :, :]


def attend(seen, queries, grads, cosine, sine, blocks, prompts):
    rows = queries.shape[0]
    wide = blocks[0].shape[1]
    few, half = prompts[0].shape[0], prompts[2].shape[0]
    keys = SPAN * rows + 4 * few + 2 * half
    part = half + 2 * few
    head = pl.BlockSpec((rows, GROUP * HD), lambda i, s: (0, i))
    outs = [(rows, f32), (rows, bf16), (rows, f32), (rows + part, f32), (part, f32)]
    return pl.pallas_call(
        attend_kernel,
        grid_spec=pltpu.PrefetchScalarGridSpec(
            num_scalar_prefetch=1,
            grid=(KVH,),
            in_specs=[head, head] + [IN_VMEM] * 10,
            out_specs=[head, head] + [IN_VMEM] * 5,
            scratch_shapes=[pltpu.VMEM((keys, HD), bf16)] * 2
            + [pltpu.VMEM((keys, HD), f32)] * 2
            + [pltpu.VMEM((2 * part, HD), f32)],
        ),
        out_shape=[jax.ShapeDtypeStruct(queries.shape, bf16)] * 2
        + [jax.ShapeDtypeStruct((r, wide), t) for r, t in outs],
        compiler_params=pltpu.CompilerParams(vmem_limit_bytes=40 * 2**20),
        name="attend",
    )(seen, in_hbm(queries), in_hbm(grads), cosine, sine, *blocks, *prompts)


def merge_kernel(d2_ref, r3_ref, dp_ref, xk_ref, xv_ref, keep_ref, *outs):
    rows, few = d2_ref.shape[0], keep_ref.shape[0]
    x2 = (d2_ref[...] + r3_ref[:rows, :]).astype(bf16)
    xk_ref[:rows, :] = x2[:, :WIDTH]
    xv_ref[:rows, :] = x2[:, WIDTH:]
    keep_ref[...] = dp_ref[:few, :] + r3_ref[rows : rows + few, :]
    near = dp_ref[few : 2 * few, :] + r3_ref[rows + few : rows + 2 * few, :]
    high = near.astype(bf16).astype(f32)
    pair = jnp.concatenate([high, near - high], axis=0).astype(bf16)
    xk_ref[rows:, :] = pair[:, :WIDTH]
    xv_ref[rows:, :] = pair[:, WIDTH:]
    for j, out in enumerate(outs):
        step = out.shape[0]
        at = 2 * few + j * step
        out[...] = dp_ref[at : at + step, :] + r3_ref[rows + at : rows + at + step, :]


def merge(d2, r3, dp, few, pieces):
    rows, wide = d2.shape
    return pl.pallas_call(
        merge_kernel,
        in_specs=[IN_VMEM] * 3,
        out_specs=[IN_VMEM] * (3 + pieces),
        out_shape=[
            jax.ShapeDtypeStruct((rows + 2 * few, WIDTH), bf16),
            jax.ShapeDtypeStruct((rows + 2 * few, WIDTH), bf16),
            jax.ShapeDtypeStruct((few, wide), f32),
        ]
        + [jax.ShapeDtypeStruct((2 * few, wide), f32)] * pieces,
        compiler_params=pltpu.CompilerParams(vmem_limit_bytes=6 * 2**20),
        name="merge",
    )(d2, r3, dp)


def tally_kernel(after_ref, *refs):
    terms, keep_ref, send_ref = refs[:-2], refs[-2], refs[-1]
    few = keep_ref.shape[0]
    total = terms[0][...]
    for term in terms[1:]:
        total = total + term[...]
    keep_ref[...] = total[:few]
    send_ref[...] = total[few:]


def tally(after, terms):
    few, wide = terms[0].shape
    return pl.pallas_call(
        tally_kernel,
        in_specs=[IN_VMEM] * (1 + len(terms)),
        out_specs=[IN_VMEM] * 2,
        out_shape=[jax.ShapeDtypeStruct((few // 2, wide), f32)] * 2,
        compiler_params=pltpu.CompilerParams(vmem_limit_bytes=2 * 2**20),
        name="tally",
    )(after, *terms)


def finish_kernel(
    d0_ref, r1_ref, rk_ref, rv_ref, cos_ref, sin_ref, keep_ref, sum_ref, got_ref,
    gk_ref, gv_ref, gpk_ref, gpv_ref,
):
    rows = d0_ref.shape[0]
    cosine, sine = cos_ref[:rows, :], -sin_ref[:rows, :]
    few = keep_ref.shape[0]
    mine = slice(SPAN * rows, SPAN * rows + 2 * few)
    pcos, psin = cos_ref[mine, :][:few], -sin_ref[mine, :][:few]
    for h in range(KVH):
        at = slice(h * HD, (h + 1) * HD)
        vat = slice(WIDTH + h * HD, WIDTH + (h + 1) * HD)
        for cols, r2_ref, out in ((at, rk_ref, gk_ref), (vat, rv_ref, gv_ref)):
            total = d0_ref[:, cols] + (r1_ref[:, cols].astype(f32) + r2_ref[:rows, at].astype(f32))
            out[:, at] = (turn(total, cosine, sine) if out is gk_ref else total).astype(bf16)
        for cols, r2_ref, out in ((at, rk_ref, gpk_ref), (vat, rv_ref, gpv_ref)):
            pair = r2_ref[rows:, at].astype(f32)
            total = keep_ref[:, cols] + (pair[:few] + pair[few:])
            total = total + (sum_ref[:, cols] + got_ref[:, cols])
            out[:, at] = (turn(total, pcos, psin) if out is gpk_ref else total).astype(bf16)


def finish(d0, r1, rk, rv, cosine, sine, keep, tallied, got):
    rows, few = d0.shape[0], keep.shape[0]
    return pl.pallas_call(
        finish_kernel,
        in_specs=[IN_VMEM] * 9,
        out_shape=[jax.ShapeDtypeStruct((r, WIDTH), bf16) for r in (rows, rows, few, few)],
        compiler_params=pltpu.CompilerParams(vmem_limit_bytes=6 * 2**20),
        name="finish",
    )(d0, r1, rk, rv, cosine, sine, keep, tallied, got)


def local(
    queries, answer_keys, answer_values, prompt_keys, prompt_values, positions, ancestry, out_grad
):
    n = lax.axis_size("ctx")
    chips = n // 2
    rows = queries.shape[0]
    few = prompt_keys.shape[0]
    me = lax.axis_index("ctx")
    core = me & 1
    swap = [(i, i ^ 1) for i in range(n)]
    ahead = [(i, (i + 2) % n) for i in range(n)]
    across = [(i, i + 1) for i in range(0, n, 2)] + [(i, i + 3) for i in range(1, n - 3, 2)]
    turns = chips // 2 - 1
    reach = [(1 + j, 1 + j + turns) for j in range(1, turns + 1)]
    rounds = [[(i, (i + 2 * k[i % 2]) % n) for i in range(n)] for k in reach]

    own, mine = pack(answer_keys, answer_values, prompt_keys, prompt_values)
    w2 = permute(own, ahead)
    w1 = permute(own, across)
    theirs = permute(mine, swap)
    chip = jnp.concatenate([mine, theirs], axis=0)
    near = jnp.concatenate([permute(chip, pairs) for pairs in rounds], axis=0)
    w3 = permute(w2, swap)
    far = permute(near, swap)

    table = ancestry[0]
    column = jnp.arange(table.shape[0], dtype=jnp.int32)[None, :]
    steps = jnp.arange(SPAN, dtype=jnp.int32)
    steps = jnp.where((core == 0) & (steps > 0), SPAN - steps, steps)
    first = me - steps
    seen = jnp.sum(jnp.where(column == first[:, None], table[None, :], 0), axis=1)
    apart = jnp.sum(
        jnp.where((column >= first[:, None]) & (column < me), table[None, :], 0), axis=1
    )
    places = (positions[None, :] - rows * apart[:, None]).reshape(-1)
    low = jnp.array([k[0] for k in reach], dtype=jnp.int32)
    high = jnp.array([k[1] for k in reach], dtype=jnp.int32)
    away = jnp.concatenate(
        [jnp.array([0, 1], jnp.int32), jnp.where(core == 0, low, high), jnp.where(core == 0, high, low)]
    )
    first_core = jnp.concatenate([jnp.full((2 + turns,), core), jnp.full((turns,), 1 - core)])
    homes = 2 * ((me // 2 - away + chips) % chips)
    homes = jnp.stack([homes + first_core, homes + 1 - first_core], axis=1)
    prompt_places = homes[:, :, None] * few + jnp.arange(few, dtype=jnp.int32)
    cosine, sine = angle_tables(jnp.concatenate([places, prompt_places.reshape(-1)]))

    attended, grad_queries, d0, d1, d2, d3, dp = attend(
        seen[1:], queries, out_grad, cosine, sine, [own, w1, w2, w3], [mine, theirs, near, far]
    )
    r3 = permute(d3, swap)
    r1 = permute(d1, back(across))
    xk, xv, keep, *terms = merge(d2, r3, dp, few, turns)
    rk = permute(xk, back(ahead))
    sums = [permute(t, back(p)) for t, p in zip(terms, rounds)]
    rv = permute(lax.optimization_barrier((xv, *sums))[0], back(ahead))
    tallied, send = tally(r1, sums)
    got = permute(send, swap)
    grad_keys, grad_values, grad_prompt_keys, grad_prompt_values = finish(
        d0, r1, rk, rv, cosine, sine, keep, tallied, got
    )
    return (attended, grad_queries, grad_keys, grad_values, grad_prompt_keys, grad_prompt_values)


def solution(mesh):
    rows = P(("groups", "ctx"), None)
    return jax.shard_map(
        local,
        mesh=mesh,
        in_specs=(rows, rows, rows, rows, rows, P(("groups", "ctx")), rows, rows),
        out_specs=(rows,) * 6,
        check_vma=False,
    )
```

```python
import jax
import jax.numpy as jnp
from jax import lax
from jax.experimental import pallas as pl
from jax.experimental.pallas import tpu as pltpu
from jax.sharding import PartitionSpec as P

QH = 20
KVH = 4
GROUP = QH // KVH
HD = 128
WIDTH = KVH * HD
SPAN = 4
SCALE = HD**-0.5
LOG2E = 1.4426950408889634
HIDDEN = -1e30

rope_base = 1000000.0

f32 = jnp.float32
bf16 = jnp.bfloat16


def in_hbm(value):
    return pltpu.with_memory_space_constraint(value, pltpu.HBM)


def permute(value, pairs):
    return lax.ppermute(value, "ctx", pairs)


def back(pairs):
    return [(b, a) for a, b in pairs]


def angle_tables(places):
    lane = jnp.arange(HD, dtype=jnp.int32)
    freqs = rope_base ** (-(2.0 * (lane % (HD // 2)).astype(f32)) / HD)
    angles = places.astype(f32)[:, None] * freqs[None, :]
    sign = jnp.where(lane < HD // 2, -1.0, 1.0).astype(f32)
    return jnp.cos(angles), jnp.sin(angles) * sign[None, :]


def dot(a, b, ca, cb):
    return lax.dot_general(a, b, (((ca,), (cb,)), ((), ())), preferred_element_type=f32)


def turn(x, cosine, sine):
    return x * cosine + pltpu.roll(x, HD // 2, 1) * sine


IN_VMEM = pl.BlockSpec(memory_space=pltpu.VMEM)
IN_HBM = pl.BlockSpec(memory_space=pltpu.HBM)


def pack_kernel(k_ref, v_ref, pk_ref, pv_ref, own_ref, mine_ref, sems):
    rows = k_ref.shape[0]
    copies = [
        pltpu.make_async_copy(src, dst, sems.at[i])
        for i, (src, dst) in enumerate(
            (
                (pk_ref, mine_ref.at[:, :WIDTH]),
                (pv_ref, mine_ref.at[:, WIDTH:]),
                (k_ref, own_ref.at[:rows, :WIDTH]),
                (v_ref, own_ref.at[:rows, WIDTH:]),
            )
        )
    ]
    for copy in copies:
        copy.start()
    copies[0].wait()
    copies[1].wait()
    twice = jnp.concatenate([mine_ref[...].astype(f32)] * 2, axis=0)
    own_ref[rows:, :] = twice.astype(bf16)
    copies[2].wait()
    copies[3].wait()


def pack(keys, values, prompt_keys, prompt_values):
    rows = keys.shape[0] + 2 * prompt_keys.shape[0]
    return pl.pallas_call(
        pack_kernel,
        in_specs=[IN_HBM] * 4,
        out_shape=[
            jax.ShapeDtypeStruct((rows, 2 * WIDTH), bf16),
            jax.ShapeDtypeStruct((prompt_keys.shape[0], 2 * WIDTH), bf16),
        ],
        out_specs=[IN_VMEM, IN_VMEM],
        scratch_shapes=[pltpu.SemaphoreType.DMA((4,))],
        compiler_params=pltpu.CompilerParams(vmem_limit_bytes=4 * 2**20),
        name="pack",
    )(*(in_hbm(x) for x in (keys, values, prompt_keys, prompt_values)))


def gather_kernel(near_ref, far_ref, out_ref):
    both = jnp.concatenate([near_ref[...].astype(f32), far_ref[...].astype(f32)], axis=0)
    out_ref[...] = both.astype(bf16)


def gather(near, far):
    half, wide = near.shape
    return pl.pallas_call(
        gather_kernel,
        in_specs=[IN_VMEM] * 2,
        out_specs=IN_VMEM,
        out_shape=jax.ShapeDtypeStruct((2 * half, wide), bf16),
        compiler_params=pltpu.CompilerParams(vmem_limit_bytes=2 * 2**20),
        name="gather",
    )(near, far)


def attend_kernel(
    seen, q_ref, g_ref, cos_ref, sin_ref, own_ref, w1_ref, w2_ref, w3_ref,
    mine_ref, theirs_ref, others_ref,
    o_ref, dq_ref, d0_ref, d1_ref, d2_ref, d3_ref, dp_ref,
    k_buf, v_buf, dk_buf, dv_buf, p_buf,
):
    rows = q_ref.shape[0]
    few, half = mine_ref.shape[0], others_ref.shape[0] // 2
    col = pl.program_id(0) * HD
    k_at = pl.ds(pl.multiple_of(col, HD), HD)
    v_at = pl.ds(pl.multiple_of(col + WIDTH, HD), HD)
    for j, part in enumerate((own_ref, w1_ref, w2_ref, w3_ref)):
        span = slice(j * rows, (j + 1) * rows)
        raw = part[:rows, k_at].astype(f32)
        k_buf[span, :] = turn(raw, cos_ref[span, :], sin_ref[span, :]).astype(bf16)
        v_buf[span, :] = part[:rows, v_at]
    span = slice(SPAN * rows, SPAN * rows + 4 * few + 2 * half)

    def prompt(at):
        p_buf[:few, :] = mine_ref[:, at].astype(f32)
        p_buf[few : 2 * few, :] = theirs_ref[:, at].astype(f32)
        p_buf[2 * few : 3 * few, :] = w2_ref[rows:, at].astype(f32)[:few]
        p_buf[3 * few : 4 * few, :] = w3_ref[rows:, at].astype(f32)[:few]
        p_buf[4 * few :, :] = others_ref[:, at].astype(f32)
        return p_buf[...]

    k_buf[span, :] = turn(prompt(k_at), cos_ref[span, :], sin_ref[span, :]).astype(bf16)
    v_buf[span, :] = prompt(v_at).astype(bf16)
    k, v = k_buf[...], v_buf[...]
    cosine, sine = cos_ref[:rows, :], sin_ref[:rows, :]
    lower = lax.broadcasted_iota(jnp.int32, (rows, rows), 1) <= lax.broadcasted_iota(
        jnp.int32, (rows, rows), 0
    )
    bias = [jnp.where(seen[i] > 0, 0.0, HIDDEN).astype(f32) for i in range(3)]

    def cols(h):
        return slice(h * HD, (h + 1) * HD)

    def open_head(h):
        q = turn(q_ref[:, cols(h)].astype(f32), cosine, sine).astype(bf16)
        g = g_ref[:, cols(h)]
        return q, g, dot(q, k, 1, 1), dot(g, v, 1, 1)

    def weigh(s):
        s_own = jnp.where(lower, s[:, :rows], HIDDEN)
        s_win = [s[:, rows * (i + 1) : rows * (i + 2)] for i in range(3)]
        s_pr = s[:, SPAN * rows :]
        peak = jnp.maximum(
            jnp.max(s_own, axis=1, keepdims=True), jnp.max(s_pr, axis=1, keepdims=True)
        )
        for i in range(3):
            peak = jnp.maximum(peak, jnp.max(s_win[i], axis=1, keepdims=True) + bias[i])
        base = peak * (SCALE * LOG2E)
        e = (
            [jnp.exp2(s_own * (SCALE * LOG2E) - base)]
            + [jnp.exp2(s_win[i] * (SCALE * LOG2E) - (base - bias[i])) for i in range(3)]
            + [jnp.exp2(s_pr * (SCALE * LOG2E) - base)]
        )
        total = sum(jnp.sum(x, axis=1, keepdims=True) for x in e)
        return jnp.concatenate(e, axis=1) * (1.0 / total)

    def close_head(h, ds, wb, q, g):
        dq_ref[:, cols(h)] = turn(dot(ds, k, 1, 0), cosine, -sine).astype(bf16)
        dk, dv = dot(ds, q, 0, 0), dot(wb, g, 0, 0)
        if h == 0:
            dk_buf[...] = dk
            dv_buf[...] = dv
        else:
            dk_buf[...] += dk
            dv_buf[...] += dv

    ahead, behind = open_head(0), None
    for h in range(GROUP):
        q, g, s, dw = ahead
        if h + 1 < GROUP:
            ahead = open_head(h + 1)
        if behind is not None:
            close_head(*behind)
        w = weigh(s)
        wb = w.astype(bf16)
        o = dot(wb, v, 1, 0).astype(bf16)
        o_ref[:, cols(h)] = o
        delta = jnp.sum(o.astype(f32) * g.astype(f32), axis=1, keepdims=True)
        behind = (h, (w * (dw - delta) * SCALE).astype(bf16), wb, q, g)
    close_head(*behind)

    start = SPAN * rows
    for at, buf in ((k_at, dk_buf), (v_at, dv_buf)):
        for j, out in enumerate((d0_ref, d1_ref, d2_ref, d3_ref)):
            out[:rows, at] = buf[j * rows : (j + 1) * rows, :].astype(out.dtype)
        for j in range(2):
            mid = start + 2 * few * j
            dp_ref[j * few : (j + 1) * few, at] = buf[mid : mid + few, :]
            d3_ref[rows + j * few : rows + (j + 1) * few, at] = buf[mid + few : mid + 2 * few, :]
        mid = start + 4 * few
        dp_ref[2 * few :, at] = buf[mid : mid + half, :]
        d3_ref[rows + 2 * few :, at] = buf[mid + half :, :]


def attend(seen, queries, grads, cosine, sine, blocks, prompts):
    rows = queries.shape[0]
    wide = blocks[0].shape[1]
    few, half = prompts[0].shape[0], prompts[2].shape[0] // 2
    keys = SPAN * rows + 4 * few + 2 * half
    part = half + 2 * few
    head = pl.BlockSpec((rows, GROUP * HD), lambda i, s: (0, i))
    outs = [(rows, f32), (rows, bf16), (rows, f32), (rows + part, f32), (part, f32)]
    return pl.pallas_call(
        attend_kernel,
        grid_spec=pltpu.PrefetchScalarGridSpec(
            num_scalar_prefetch=1,
            grid=(KVH,),
            in_specs=[head, head] + [IN_VMEM] * 9,
            out_specs=[head, head] + [IN_VMEM] * 5,
            scratch_shapes=[pltpu.VMEM((keys, HD), bf16)] * 2
            + [pltpu.VMEM((keys, HD), f32)] * 2
            + [pltpu.VMEM((2 * part, HD), f32)],
        ),
        out_shape=[jax.ShapeDtypeStruct(queries.shape, bf16)] * 2
        + [jax.ShapeDtypeStruct((r, wide), t) for r, t in outs],
        compiler_params=pltpu.CompilerParams(vmem_limit_bytes=40 * 2**20),
        name="attend",
    )(seen, in_hbm(queries), in_hbm(grads), cosine, sine, *blocks, *prompts)


def merge_kernel(d2_ref, r3_ref, dp_ref, xk_ref, xv_ref, keep_ref, *outs):
    rows, few = d2_ref.shape[0], keep_ref.shape[0]
    x2 = (d2_ref[...] + r3_ref[:rows, :]).astype(bf16)
    xk_ref[:rows, :] = x2[:, :WIDTH]
    xv_ref[:rows, :] = x2[:, WIDTH:]
    keep_ref[...] = dp_ref[:few, :] + r3_ref[rows : rows + few, :]
    near = dp_ref[few : 2 * few, :] + r3_ref[rows + few : rows + 2 * few, :]
    high = near.astype(bf16).astype(f32)
    pair = jnp.concatenate([high, near - high], axis=0).astype(bf16)
    xk_ref[rows:, :] = pair[:, :WIDTH]
    xv_ref[rows:, :] = pair[:, WIDTH:]
    for j, out in enumerate(outs):
        step = out.shape[0]
        at = 2 * few + j * step
        out[...] = dp_ref[at : at + step, :] + r3_ref[rows + at : rows + at + step, :]


def merge(d2, r3, dp, few, pieces):
    rows, wide = d2.shape
    return pl.pallas_call(
        merge_kernel,
        in_specs=[IN_VMEM] * 3,
        out_specs=[IN_VMEM] * (3 + pieces),
        out_shape=[
            jax.ShapeDtypeStruct((rows + 2 * few, WIDTH), bf16),
            jax.ShapeDtypeStruct((rows + 2 * few, WIDTH), bf16),
            jax.ShapeDtypeStruct((few, wide), f32),
        ]
        + [jax.ShapeDtypeStruct((2 * few, wide), f32)] * pieces,
        compiler_params=pltpu.CompilerParams(vmem_limit_bytes=6 * 2**20),
        name="merge",
    )(d2, r3, dp)


def tally_kernel(after_ref, later_ref, *refs):
    terms, keep_ref, send_ref = refs[:-2], refs[-2], refs[-1]
    few = keep_ref.shape[0]
    total = terms[0][...]
    for term in terms[1:]:
        total = total + term[...]
    keep_ref[...] = total[:few]
    send_ref[...] = total[few:]


def tally(after, later, terms):
    few, wide = terms[0].shape
    return pl.pallas_call(
        tally_kernel,
        in_specs=[IN_VMEM] * (2 + len(terms)),
        out_specs=[IN_VMEM] * 2,
        out_shape=[jax.ShapeDtypeStruct((few // 2, wide), f32)] * 2,
        compiler_params=pltpu.CompilerParams(vmem_limit_bytes=2 * 2**20),
        name="tally",
    )(after, later, *terms)


def finish_kernel(
    d0_ref, r1_ref, rk_ref, rv_ref, cos_ref, sin_ref, keep_ref, sum_ref, got_ref,
    gk_ref, gv_ref, gpk_ref, gpv_ref,
):
    rows = d0_ref.shape[0]
    cosine, sine = cos_ref[:rows, :], -sin_ref[:rows, :]
    few = keep_ref.shape[0]
    mine = slice(SPAN * rows, SPAN * rows + 2 * few)
    pcos, psin = cos_ref[mine, :][:few], -sin_ref[mine, :][:few]
    for h in range(KVH):
        at = slice(h * HD, (h + 1) * HD)
        vat = slice(WIDTH + h * HD, WIDTH + (h + 1) * HD)
        for cols, r2_ref, out in ((at, rk_ref, gk_ref), (vat, rv_ref, gv_ref)):
            total = d0_ref[:, cols] + (r1_ref[:, cols].astype(f32) + r2_ref[:rows, at].astype(f32))
            out[:, at] = (turn(total, cosine, sine) if out is gk_ref else total).astype(bf16)
        for cols, r2_ref, out in ((at, rk_ref, gpk_ref), (vat, rv_ref, gpv_ref)):
            pair = r2_ref[rows:, at].astype(f32)
            total = keep_ref[:, cols] + (pair[:few] + pair[few:])
            total = total + (sum_ref[:, cols] + got_ref[:, cols])
            out[:, at] = (turn(total, pcos, psin) if out is gpk_ref else total).astype(bf16)


def finish(d0, r1, rk, rv, cosine, sine, keep, tallied, got):
    rows, few = d0.shape[0], keep.shape[0]
    return pl.pallas_call(
        finish_kernel,
        in_specs=[IN_VMEM] * 9,
        out_shape=[jax.ShapeDtypeStruct((r, WIDTH), bf16) for r in (rows, rows, few, few)],
        compiler_params=pltpu.CompilerParams(vmem_limit_bytes=6 * 2**20),
        name="finish",
    )(d0, r1, rk, rv, cosine, sine, keep, tallied, got)


def local(
    queries, answer_keys, answer_values, prompt_keys, prompt_values, positions, ancestry, out_grad
):
    n = lax.axis_size("ctx")
    chips = n // 2
    rows = queries.shape[0]
    few = prompt_keys.shape[0]
    me = lax.axis_index("ctx")
    core = me & 1
    swap = [(i, i ^ 1) for i in range(n)]
    ahead = [(i, (i + 2) % n) for i in range(n)]
    across = [(i, i + 1) for i in range(0, n, 2)] + [(i, i + 3) for i in range(1, n - 3, 2)]
    turns = chips // 2 - 1
    reach = [(1 + j, 1 + j + turns) for j in range(1, turns + 1)]
    rounds = [[(i, (i + 2 * k[i % 2]) % n) for i in range(n)] for k in reach]

    own, mine = pack(answer_keys, answer_values, prompt_keys, prompt_values)
    w2 = permute(own, ahead)
    theirs = permute(mine, swap)
    chip = jnp.concatenate([mine, theirs], axis=0)
    w1 = permute(lax.optimization_barrier((own, chip))[0], across)
    near = jnp.concatenate([permute(chip, pairs) for pairs in rounds], axis=0)
    w3 = permute(w2, swap)
    others = gather(near, permute(near, swap))

    table = ancestry[0]
    column = jnp.arange(table.shape[0], dtype=jnp.int32)[None, :]
    steps = jnp.arange(SPAN, dtype=jnp.int32)
    steps = jnp.where((core == 0) & (steps > 0), SPAN - steps, steps)
    first = me - steps
    seen = jnp.sum(jnp.where(column == first[:, None], table[None, :], 0), axis=1)
    apart = jnp.sum(
        jnp.where((column >= first[:, None]) & (column < me), table[None, :], 0), axis=1
    )
    places = (positions[None, :] - rows * apart[:, None]).reshape(-1)
    low = jnp.array([k[0] for k in reach], dtype=jnp.int32)
    high = jnp.array([k[1] for k in reach], dtype=jnp.int32)
    away = jnp.concatenate(
        [jnp.array([0, 1], jnp.int32), jnp.where(core == 0, low, high), jnp.where(core == 0, high, low)]
    )
    first_core = jnp.concatenate([jnp.full((2 + turns,), core), jnp.full((turns,), 1 - core)])
    homes = 2 * ((me // 2 - away + chips) % chips)
    homes = jnp.stack([homes + first_core, homes + 1 - first_core], axis=1)
    prompt_places = homes[:, :, None] * few + jnp.arange(few, dtype=jnp.int32)
    cosine, sine = angle_tables(jnp.concatenate([places, prompt_places.reshape(-1)]))

    attended, grad_queries, d0, d1, d2, d3, dp = attend(
        seen[1:], queries, out_grad, cosine, sine, [own, w1, w2, w3], [mine, theirs, others]
    )
    r3 = permute(d3, swap)
    r1 = permute(d1, back(across))
    xk, xv, keep, *terms = merge(d2, r3, dp, few, turns)
    rk = permute(xk, back(ahead))
    sums = [permute(t, back(p)) for t, p in zip(terms, rounds)]
    rv = permute(lax.optimization_barrier((xv, r1, rk, *sums))[0], back(ahead))
    tallied, send = tally(r1, rk, sums)
    got = permute(send, swap)
    grad_keys, grad_values, grad_prompt_keys, grad_prompt_values = finish(
        d0, r1, rk, rv, cosine, sine, keep, tallied, got
    )
    return (attended, grad_queries, grad_keys, grad_values, grad_prompt_keys, grad_prompt_values)


def solution(mesh):
    rows = P(("groups", "ctx"), None)
    return jax.shard_map(
        local,
        mesh=mesh,
        in_specs=(rows, rows, rows, rows, rows, P(("groups", "ctx")), rows, rows),
        out_specs=(rows,) * 6,
        check_vma=False,
    )
```

```python
import jax
import jax.numpy as jnp
from jax import lax
from jax.experimental import pallas as pl
from jax.experimental.pallas import tpu as pltpu
from jax.sharding import PartitionSpec as P

QH = 20
KVH = 4
GROUP = QH // KVH
PAIR = 2
HD = 128
WIDTH = KVH * HD
SPAN = 4
SCALE = HD**-0.5
LOG2E = 1.4426950408889634
HIDDEN = -1e30

rope_base = 1000000.0

f32 = jnp.float32
bf16 = jnp.bfloat16


def in_hbm(value):
    return pltpu.with_memory_space_constraint(value, pltpu.HBM)


def permute(value, pairs):
    return lax.ppermute(value, "ctx", pairs)


def back(pairs):
    return [(b, a) for a, b in pairs]


def angle_tables(places):
    lane = jnp.arange(HD, dtype=jnp.int32)
    freqs = rope_base ** (-(2.0 * (lane % (HD // 2)).astype(f32)) / HD)
    angles = places.astype(f32)[:, None] * freqs[None, :]
    sign = jnp.where(lane < HD // 2, -1.0, 1.0).astype(f32)
    return jnp.cos(angles), jnp.sin(angles) * sign[None, :]


def dot(a, b, ca, cb):
    return lax.dot_general(a, b, (((ca,), (cb,)), ((), ())), preferred_element_type=f32)


def turn(x, cosine, sine):
    return x * cosine + pltpu.roll(x, HD // 2, 1) * sine


IN_VMEM = pl.BlockSpec(memory_space=pltpu.VMEM)
IN_HBM = pl.BlockSpec(memory_space=pltpu.HBM)


def pack_kernel(k_ref, v_ref, pk_ref, pv_ref, own_ref, mine_ref, sems):
    rows = k_ref.shape[0]
    copies = [
        pltpu.make_async_copy(src, dst, sems.at[i])
        for i, (src, dst) in enumerate(
            (
                (pk_ref, mine_ref.at[:, :WIDTH]),
                (pv_ref, mine_ref.at[:, WIDTH:]),
                (k_ref, own_ref.at[:rows, :WIDTH]),
                (v_ref, own_ref.at[:rows, WIDTH:]),
            )
        )
    ]
    for copy in copies:
        copy.start()
    copies[0].wait()
    copies[1].wait()
    twice = jnp.concatenate([mine_ref[...].astype(f32)] * 2, axis=0)
    own_ref[rows:, :] = twice.astype(bf16)
    copies[2].wait()
    copies[3].wait()


def pack(keys, values, prompt_keys, prompt_values):
    rows = keys.shape[0] + 2 * prompt_keys.shape[0]
    return pl.pallas_call(
        pack_kernel,
        in_specs=[IN_HBM] * 4,
        out_shape=[
            jax.ShapeDtypeStruct((rows, 2 * WIDTH), bf16),
            jax.ShapeDtypeStruct((prompt_keys.shape[0], 2 * WIDTH), bf16),
        ],
        out_specs=[IN_VMEM, IN_VMEM],
        scratch_shapes=[pltpu.SemaphoreType.DMA((4,))],
        compiler_params=pltpu.CompilerParams(vmem_limit_bytes=4 * 2**20),
        name="pack",
    )(*(in_hbm(x) for x in (keys, values, prompt_keys, prompt_values)))


def gather_kernel(near_ref, far_ref, out_ref):
    both = jnp.concatenate([near_ref[...].astype(f32), far_ref[...].astype(f32)], axis=0)
    out_ref[...] = both.astype(bf16)


def gather(near, far):
    half, wide = near.shape
    return pl.pallas_call(
        gather_kernel,
        in_specs=[IN_VMEM] * 2,
        out_specs=IN_VMEM,
        out_shape=jax.ShapeDtypeStruct((2 * half, wide), bf16),
        compiler_params=pltpu.CompilerParams(vmem_limit_bytes=2 * 2**20),
        name="gather",
    )(near, far)


def attend_kernel(
    seen, q_ref, g_ref, cos_ref, sin_ref, own_ref, w1_ref, w2_ref, w3_ref,
    mine_ref, theirs_ref, others_ref,
    o_ref, dq_ref, d0_ref, d1_ref, d2_ref, d3_ref, dp_ref,
    k_buf, v_buf, dk_buf, dv_buf, p_buf,
):
    rows = q_ref.shape[0]
    few, half = mine_ref.shape[0], others_ref.shape[0] // 2
    col = pl.program_id(0) * (PAIR * HD)
    k_at = [pl.ds(pl.multiple_of(col + p * HD, HD), HD) for p in range(PAIR)]
    v_at = [pl.ds(pl.multiple_of(col + p * HD + WIDTH, HD), HD) for p in range(PAIR)]
    for p in range(PAIR):
        for j, part in enumerate((own_ref, w1_ref, w2_ref, w3_ref)):
            span = slice(j * rows, (j + 1) * rows)
            raw = part[:rows, k_at[p]].astype(f32)
            k_buf[p, span, :] = turn(raw, cos_ref[span, :], sin_ref[span, :]).astype(bf16)
            v_buf[p, span, :] = part[:rows, v_at[p]]
    span = slice(SPAN * rows, SPAN * rows + 4 * few + 2 * half)

    def prompt(at):
        p_buf[:few, :] = mine_ref[:, at].astype(f32)
        p_buf[few : 2 * few, :] = theirs_ref[:, at].astype(f32)
        p_buf[2 * few : 3 * few, :] = w2_ref[rows:, at].astype(f32)[:few]
        p_buf[3 * few : 4 * few, :] = w3_ref[rows:, at].astype(f32)[:few]
        p_buf[4 * few :, :] = others_ref[:, at].astype(f32)
        return p_buf[...]

    for p in range(PAIR):
        k_buf[p, span, :] = turn(prompt(k_at[p]), cos_ref[span, :], sin_ref[span, :]).astype(bf16)
        v_buf[p, span, :] = prompt(v_at[p]).astype(bf16)
    keys, vals = [k_buf[p] for p in range(PAIR)], [v_buf[p] for p in range(PAIR)]
    cosine, sine = cos_ref[:rows, :], sin_ref[:rows, :]
    lower = lax.broadcasted_iota(jnp.int32, (rows, rows), 1) <= lax.broadcasted_iota(
        jnp.int32, (rows, rows), 0
    )
    bias = [jnp.where(seen[i] > 0, 0.0, HIDDEN).astype(f32) for i in range(3)]

    def cols(h):
        return slice(h * HD, (h + 1) * HD)

    def open_head(h):
        q = turn(q_ref[:, cols(h)].astype(f32), cosine, sine).astype(bf16)
        g = g_ref[:, cols(h)]
        return q, g, dot(q, keys[h // GROUP], 1, 1), dot(g, vals[h // GROUP], 1, 1)

    def weigh(s):
        s_own = jnp.where(lower, s[:, :rows], HIDDEN)
        s_win = [s[:, rows * (i + 1) : rows * (i + 2)] for i in range(3)]
        s_pr = s[:, SPAN * rows :]
        peak = jnp.maximum(
            jnp.max(s_own, axis=1, keepdims=True), jnp.max(s_pr, axis=1, keepdims=True)
        )
        for i in range(3):
            peak = jnp.maximum(peak, jnp.max(s_win[i], axis=1, keepdims=True) + bias[i])
        base = peak * (SCALE * LOG2E)
        e = (
            [jnp.exp2(s_own * (SCALE * LOG2E) - base)]
            + [jnp.exp2(s_win[i] * (SCALE * LOG2E) - (base - bias[i])) for i in range(3)]
            + [jnp.exp2(s_pr * (SCALE * LOG2E) - base)]
        )
        total = sum(jnp.sum(x, axis=1, keepdims=True) for x in e)
        return jnp.concatenate(e, axis=1) * (1.0 / total)

    def close_head(h, ds, wb, q, g):
        dq_ref[:, cols(h)] = turn(dot(ds, keys[h // GROUP], 1, 0), cosine, -sine).astype(bf16)
        dk, dv = dot(ds, q, 0, 0), dot(wb, g, 0, 0)
        p = h // GROUP
        if h % GROUP == 0:
            dk_buf[p] = dk
            dv_buf[p] = dv
        else:
            dk_buf[p] += dk
            dv_buf[p] += dv

    ahead, behind = open_head(0), None
    for h in range(PAIR * GROUP):
        q, g, s, dw = ahead
        if h + 1 < PAIR * GROUP:
            ahead = open_head(h + 1)
        if behind is not None:
            close_head(*behind)
        w = weigh(s)
        wb = w.astype(bf16)
        o = dot(wb, vals[h // GROUP], 1, 0).astype(bf16)
        o_ref[:, cols(h)] = o
        delta = jnp.sum(o.astype(f32) * g.astype(f32), axis=1, keepdims=True)
        behind = (h, (w * (dw - delta) * SCALE).astype(bf16), wb, q, g)
    close_head(*behind)

    start = SPAN * rows
    pairs = [(k_at[p], dk_buf.at[p]) for p in range(PAIR)]
    pairs += [(v_at[p], dv_buf.at[p]) for p in range(PAIR)]
    for at, buf in pairs:
        for j, out in enumerate((d0_ref, d1_ref, d2_ref, d3_ref)):
            out[:rows, at] = buf[j * rows : (j + 1) * rows, :].astype(out.dtype)
        for j in range(2):
            mid = start + 2 * few * j
            dp_ref[j * few : (j + 1) * few, at] = buf[mid : mid + few, :]
            d3_ref[rows + j * few : rows + (j + 1) * few, at] = buf[mid + few : mid + 2 * few, :]
        mid = start + 4 * few
        dp_ref[2 * few :, at] = buf[mid : mid + half, :]
        d3_ref[rows + 2 * few :, at] = buf[mid + half :, :]


def attend(seen, queries, grads, cosine, sine, blocks, prompts):
    rows = queries.shape[0]
    wide = blocks[0].shape[1]
    few, half = prompts[0].shape[0], prompts[2].shape[0] // 2
    keys = SPAN * rows + 4 * few + 2 * half
    part = half + 2 * few
    head = pl.BlockSpec((rows, PAIR * GROUP * HD), lambda i, s: (0, i))
    outs = [(rows, f32), (rows, bf16), (rows, f32), (rows + part, f32), (part, f32)]
    return pl.pallas_call(
        attend_kernel,
        grid_spec=pltpu.PrefetchScalarGridSpec(
            num_scalar_prefetch=1,
            grid=(KVH // PAIR,),
            in_specs=[head, head] + [IN_VMEM] * 9,
            out_specs=[head, head] + [IN_VMEM] * 5,
            scratch_shapes=[pltpu.VMEM((PAIR, keys, HD), bf16)] * 2
            + [pltpu.VMEM((PAIR, keys, HD), f32)] * 2
            + [pltpu.VMEM((2 * part, HD), f32)],
        ),
        out_shape=[jax.ShapeDtypeStruct(queries.shape, bf16)] * 2
        + [jax.ShapeDtypeStruct((r, wide), t) for r, t in outs],
        compiler_params=pltpu.CompilerParams(vmem_limit_bytes=40 * 2**20),
        name="attend",
    )(seen, in_hbm(queries), in_hbm(grads), cosine, sine, *blocks, *prompts)


def merge_kernel(d2_ref, r3_ref, dp_ref, xk_ref, xv_ref, keep_ref, *outs):
    rows, few = d2_ref.shape[0], keep_ref.shape[0]
    x2 = (d2_ref[...] + r3_ref[:rows, :]).astype(bf16)
    xk_ref[:rows, :] = x2[:, :WIDTH]
    xv_ref[:rows, :] = x2[:, WIDTH:]
    keep_ref[...] = dp_ref[:few, :] + r3_ref[rows : rows + few, :]
    near = dp_ref[few : 2 * few, :] + r3_ref[rows + few : rows + 2 * few, :]
    high = near.astype(bf16).astype(f32)
    pair = jnp.concatenate([high, near - high], axis=0).astype(bf16)
    xk_ref[rows:, :] = pair[:, :WIDTH]
    xv_ref[rows:, :] = pair[:, WIDTH:]
    for j, out in enumerate(outs):
        step = out.shape[0]
        at = 2 * few + j * step
        out[...] = dp_ref[at : at + step, :] + r3_ref[rows + at : rows + at + step, :]


def merge(d2, r3, dp, few, pieces):
    rows, wide = d2.shape
    return pl.pallas_call(
        merge_kernel,
        in_specs=[IN_VMEM] * 3,
        out_specs=[IN_VMEM] * (3 + pieces),
        out_shape=[
            jax.ShapeDtypeStruct((rows + 2 * few, WIDTH), bf16),
            jax.ShapeDtypeStruct((rows + 2 * few, WIDTH), bf16),
            jax.ShapeDtypeStruct((few, wide), f32),
        ]
        + [jax.ShapeDtypeStruct((2 * few, wide), f32)] * pieces,
        compiler_params=pltpu.CompilerParams(vmem_limit_bytes=6 * 2**20),
        name="merge",
    )(d2, r3, dp)


def tally_kernel(after_ref, later_ref, *refs):
    terms, keep_ref, send_ref = refs[:-2], refs[-2], refs[-1]
    few = keep_ref.shape[0]
    total = terms[0][...]
    for term in terms[1:]:
        total = total + term[...]
    keep_ref[...] = total[:few]
    send_ref[...] = total[few:]


def tally(after, later, terms):
    few, wide = terms[0].shape
    return pl.pallas_call(
        tally_kernel,
        in_specs=[IN_VMEM] * (2 + len(terms)),
        out_specs=[IN_VMEM] * 2,
        out_shape=[jax.ShapeDtypeStruct((few // 2, wide), f32)] * 2,
        compiler_params=pltpu.CompilerParams(vmem_limit_bytes=2 * 2**20),
        name="tally",
    )(after, later, *terms)


def finish_kernel(
    d0_ref, r1_ref, rk_ref, rv_ref, cos_ref, sin_ref, keep_ref, sum_ref, got_ref,
    gk_ref, gv_ref, gpk_ref, gpv_ref,
):
    rows = d0_ref.shape[0]
    cosine, sine = cos_ref[:rows, :], -sin_ref[:rows, :]
    few = keep_ref.shape[0]
    mine = slice(SPAN * rows, SPAN * rows + 2 * few)
    pcos, psin = cos_ref[mine, :][:few], -sin_ref[mine, :][:few]
    for h in range(KVH):
        at = slice(h * HD, (h + 1) * HD)
        vat = slice(WIDTH + h * HD, WIDTH + (h + 1) * HD)
        for cols, r2_ref, out in ((at, rk_ref, gk_ref), (vat, rv_ref, gv_ref)):
            total = d0_ref[:, cols] + (r1_ref[:, cols].astype(f32) + r2_ref[:rows, at].astype(f32))
            out[:, at] = (turn(total, cosine, sine) if out is gk_ref else total).astype(bf16)
        for cols, r2_ref, out in ((at, rk_ref, gpk_ref), (vat, rv_ref, gpv_ref)):
            pair = r2_ref[rows:, at].astype(f32)
            total = keep_ref[:, cols] + (pair[:few] + pair[few:])
            total = total + (sum_ref[:, cols] + got_ref[:, cols])
            out[:, at] = (turn(total, pcos, psin) if out is gpk_ref else total).astype(bf16)


def finish(d0, r1, rk, rv, cosine, sine, keep, tallied, got):
    rows, few = d0.shape[0], keep.shape[0]
    return pl.pallas_call(
        finish_kernel,
        in_specs=[IN_VMEM] * 9,
        out_shape=[jax.ShapeDtypeStruct((r, WIDTH), bf16) for r in (rows, rows, few, few)],
        compiler_params=pltpu.CompilerParams(vmem_limit_bytes=6 * 2**20),
        name="finish",
    )(d0, r1, rk, rv, cosine, sine, keep, tallied, got)


def local(
    queries, answer_keys, answer_values, prompt_keys, prompt_values, positions, ancestry, out_grad
):
    n = lax.axis_size("ctx")
    chips = n // 2
    rows = queries.shape[0]
    few = prompt_keys.shape[0]
    me = lax.axis_index("ctx")
    core = me & 1
    swap = [(i, i ^ 1) for i in range(n)]
    ahead = [(i, (i + 2) % n) for i in range(n)]
    across = [(i, i + 1) for i in range(0, n, 2)] + [(i, i + 3) for i in range(1, n - 3, 2)]
    turns = chips // 2 - 1
    reach = [(1 + j, 1 + j + turns) for j in range(1, turns + 1)]
    rounds = [[(i, (i + 2 * k[i % 2]) % n) for i in range(n)] for k in reach]

    own, mine = pack(answer_keys, answer_values, prompt_keys, prompt_values)
    w2 = permute(own, ahead)
    theirs = permute(mine, swap)
    chip = jnp.concatenate([mine, theirs], axis=0)
    w1 = permute(lax.optimization_barrier((own, chip))[0], across)
    near = jnp.concatenate([permute(chip, pairs) for pairs in rounds], axis=0)
    w3 = permute(w2, swap)
    others = gather(near, permute(near, swap))

    table = ancestry[0]
    column = jnp.arange(table.shape[0], dtype=jnp.int32)[None, :]
    steps = jnp.arange(SPAN, dtype=jnp.int32)
    steps = jnp.where((core == 0) & (steps > 0), SPAN - steps, steps)
    first = me - steps
    seen = jnp.sum(jnp.where(column == first[:, None], table[None, :], 0), axis=1)
    apart = jnp.sum(
        jnp.where((column >= first[:, None]) & (column < me), table[None, :], 0), axis=1
    )
    places = (positions[None, :] - rows * apart[:, None]).reshape(-1)
    low = jnp.array([k[0] for k in reach], dtype=jnp.int32)
    high = jnp.array([k[1] for k in reach], dtype=jnp.int32)
    away = jnp.concatenate(
        [jnp.array([0, 1], jnp.int32), jnp.where(core == 0, low, high), jnp.where(core == 0, high, low)]
    )
    first_core = jnp.concatenate([jnp.full((2 + turns,), core), jnp.full((turns,), 1 - core)])
    homes = 2 * ((me // 2 - away + chips) % chips)
    homes = jnp.stack([homes + first_core, homes + 1 - first_core], axis=1)
    prompt_places = homes[:, :, None] * few + jnp.arange(few, dtype=jnp.int32)
    cosine, sine = angle_tables(jnp.concatenate([places, prompt_places.reshape(-1)]))

    attended, grad_queries, d0, d1, d2, d3, dp = attend(
        seen[1:], queries, out_grad, cosine, sine, [own, w1, w2, w3], [mine, theirs, others]
    )
    r3 = permute(d3, swap)
    r1 = permute(d1, back(across))
    xk, xv, keep, *terms = merge(d2, r3, dp, few, turns)
    rk = permute(xk, back(ahead))
    sums = [permute(t, back(p)) for t, p in zip(terms, rounds)]
    rv = permute(lax.optimization_barrier((xv, r1, rk, *sums))[0], back(ahead))
    tallied, send = tally(r1, rk, sums)
    got = permute(send, swap)
    grad_keys, grad_values, grad_prompt_keys, grad_prompt_values = finish(
        d0, r1, rk, rv, cosine, sine, keep, tallied, got
    )
    return (attended, grad_queries, grad_keys, grad_values, grad_prompt_keys, grad_prompt_values)


def solution(mesh):
    rows = P(("groups", "ctx"), None)
    return jax.shard_map(
        local,
        mesh=mesh,
        in_specs=(rows, rows, rows, rows, rows, P(("groups", "ctx")), rows, rows),
        out_specs=(rows,) * 6,
        check_vma=False,
    )
```

```python
import jax
import jax.numpy as jnp
from jax import lax
from jax.experimental import pallas as pl
from jax.experimental.pallas import tpu as pltpu
from jax.sharding import PartitionSpec as P

QH = 20
KVH = 4
GROUP = QH // KVH
PAIR = 2
HD = 128
WIDTH = KVH * HD
SPAN = 4
SCALE = HD**-0.5
HIDDEN = -1e30

rope_base = 1000000.0

f32 = jnp.float32
bf16 = jnp.bfloat16


def in_hbm(value):
    return pltpu.with_memory_space_constraint(value, pltpu.HBM)


def permute(value, pairs):
    return lax.ppermute(value, "ctx", pairs)


def back(pairs):
    return [(b, a) for a, b in pairs]


def angle_tables(places):
    lane = jnp.arange(HD, dtype=jnp.int32)
    freqs = rope_base ** (-(2.0 * (lane % (HD // 2)).astype(f32)) / HD)
    angles = places.astype(f32)[:, None] * freqs[None, :]
    sign = jnp.where(lane < HD // 2, -1.0, 1.0).astype(f32)
    return jnp.cos(angles), jnp.sin(angles) * sign[None, :]


def dot(a, b, ca, cb):
    return lax.dot_general(a, b, (((ca,), (cb,)), ((), ())), preferred_element_type=f32)


def turn(x, cosine, sine):
    return x * cosine + pltpu.roll(x, HD // 2, 1) * sine


IN_VMEM = pl.BlockSpec(memory_space=pltpu.VMEM)
IN_HBM = pl.BlockSpec(memory_space=pltpu.HBM)


def pack_kernel(k_ref, v_ref, pk_ref, pv_ref, own_ref, mine_ref, sems):
    rows = k_ref.shape[0]
    copies = [
        pltpu.make_async_copy(src, dst, sems.at[i])
        for i, (src, dst) in enumerate(
            (
                (pk_ref, mine_ref.at[:, :WIDTH]),
                (pv_ref, mine_ref.at[:, WIDTH:]),
                (k_ref, own_ref.at[:rows, :WIDTH]),
                (v_ref, own_ref.at[:rows, WIDTH:]),
            )
        )
    ]
    for copy in copies:
        copy.start()
    copies[0].wait()
    copies[1].wait()
    twice = jnp.concatenate([mine_ref[...].astype(f32)] * 2, axis=0)
    own_ref[rows:, :] = twice.astype(bf16)
    copies[2].wait()
    copies[3].wait()


def pack(keys, values, prompt_keys, prompt_values):
    rows = keys.shape[0] + 2 * prompt_keys.shape[0]
    return pl.pallas_call(
        pack_kernel,
        in_specs=[IN_HBM] * 4,
        out_shape=[
            jax.ShapeDtypeStruct((rows, 2 * WIDTH), bf16),
            jax.ShapeDtypeStruct((prompt_keys.shape[0], 2 * WIDTH), bf16),
        ],
        out_specs=[IN_VMEM, IN_VMEM],
        scratch_shapes=[pltpu.SemaphoreType.DMA((4,))],
        compiler_params=pltpu.CompilerParams(vmem_limit_bytes=4 * 2**20),
        name="pack",
    )(*(in_hbm(x) for x in (keys, values, prompt_keys, prompt_values)))


def gather_kernel(near_ref, far_ref, out_ref):
    both = jnp.concatenate([near_ref[...].astype(f32), far_ref[...].astype(f32)], axis=0)
    out_ref[...] = both.astype(bf16)


def gather(near, far):
    half, wide = near.shape
    return pl.pallas_call(
        gather_kernel,
        in_specs=[IN_VMEM] * 2,
        out_specs=IN_VMEM,
        out_shape=jax.ShapeDtypeStruct((2 * half, wide), bf16),
        compiler_params=pltpu.CompilerParams(vmem_limit_bytes=2 * 2**20),
        name="gather",
    )(near, far)


def attend_kernel(
    seen, q_ref, g_ref, cos_ref, sin_ref, own_ref, w1_ref, w2_ref, w3_ref,
    mine_ref, theirs_ref, others_ref,
    o_ref, dq_ref, d0_ref, d1_ref, d2_ref, d3_ref, dp_ref,
    k_buf, v_buf, dk_buf, dv_buf, p_buf,
):
    rows = q_ref.shape[0]
    few, half = mine_ref.shape[0], others_ref.shape[0] // 2
    col = pl.program_id(0) * (PAIR * HD)
    k_at = [pl.ds(pl.multiple_of(col + p * HD, HD), HD) for p in range(PAIR)]
    v_at = [pl.ds(pl.multiple_of(col + p * HD + WIDTH, HD), HD) for p in range(PAIR)]
    for p in range(PAIR):
        for j, part in enumerate((own_ref, w1_ref, w2_ref, w3_ref)):
            span = slice(j * rows, (j + 1) * rows)
            raw = part[:rows, k_at[p]].astype(f32)
            k_buf[p, span, :] = turn(raw, cos_ref[span, :], sin_ref[span, :]).astype(bf16)
            v_buf[p, span, :] = part[:rows, v_at[p]]
    span = slice(SPAN * rows, SPAN * rows + 4 * few + 2 * half)

    def prompt(at):
        p_buf[:few, :] = mine_ref[:, at].astype(f32)
        p_buf[few : 2 * few, :] = theirs_ref[:, at].astype(f32)
        p_buf[2 * few : 3 * few, :] = w2_ref[rows:, at].astype(f32)[:few]
        p_buf[3 * few : 4 * few, :] = w3_ref[rows:, at].astype(f32)[:few]
        p_buf[4 * few :, :] = others_ref[:, at].astype(f32)
        return p_buf[...]

    for p in range(PAIR):
        k_buf[p, span, :] = turn(prompt(k_at[p]), cos_ref[span, :], sin_ref[span, :]).astype(bf16)
        v_buf[p, span, :] = prompt(v_at[p]).astype(bf16)
    keys, vals = [k_buf[p] for p in range(PAIR)], [v_buf[p] for p in range(PAIR)]
    cosine, sine = cos_ref[:rows, :], sin_ref[:rows, :]
    lower = lax.broadcasted_iota(jnp.int32, (rows, rows), 1) <= lax.broadcasted_iota(
        jnp.int32, (rows, rows), 0
    )
    bias = [jnp.where(seen[i] > 0, 0.0, HIDDEN).astype(f32) for i in range(3)]

    def cols(h):
        return slice(h * HD, (h + 1) * HD)

    def open_head(h):
        q = turn(q_ref[:, cols(h)].astype(f32), cosine, sine).astype(bf16)
        g = g_ref[:, cols(h)]
        return q, g, dot(q, keys[h // GROUP], 1, 1), dot(g, vals[h // GROUP], 1, 1)

    def weigh(s):
        s_own = jnp.where(lower, s[:, :rows], HIDDEN)
        s_win = [s[:, rows * (i + 1) : rows * (i + 2)] for i in range(3)]
        s_pr = s[:, SPAN * rows :]
        peak = jnp.maximum(
            jnp.max(s_own, axis=1, keepdims=True), jnp.max(s_pr, axis=1, keepdims=True)
        )
        for i in range(3):
            peak = jnp.maximum(peak, jnp.max(s_win[i], axis=1, keepdims=True) + bias[i])
        base = peak * SCALE
        e = (
            [jnp.exp(s_own * SCALE - base)]
            + [jnp.exp(s_win[i] * SCALE - (base - bias[i])) for i in range(3)]
            + [jnp.exp(s_pr * SCALE - base)]
        )
        total = sum(jnp.sum(x, axis=1, keepdims=True) for x in e)
        return jnp.concatenate(e, axis=1) * (1.0 / total)

    def close_head(h, ds, wb, q, g):
        dq_ref[:, cols(h)] = turn(dot(ds, keys[h // GROUP], 1, 0), cosine, -sine).astype(bf16)
        dk, dv = dot(ds, q, 0, 0), dot(wb, g, 0, 0)
        p = h // GROUP
        if h % GROUP == 0:
            dk_buf[p] = dk
            dv_buf[p] = dv
        else:
            dk_buf[p] += dk
            dv_buf[p] += dv

    ahead, behind = open_head(0), None
    for h in range(PAIR * GROUP):
        q, g, s, dw = ahead
        if h + 1 < PAIR * GROUP:
            ahead = open_head(h + 1)
        if behind is not None:
            close_head(*behind)
        w = weigh(s)
        wb = w.astype(bf16)
        o = dot(wb, vals[h // GROUP], 1, 0).astype(bf16)
        o_ref[:, cols(h)] = o
        delta = jnp.sum(o.astype(f32) * g.astype(f32), axis=1, keepdims=True)
        behind = (h, (w * (dw - delta) * SCALE).astype(bf16), wb, q, g)
    close_head(*behind)

    start = SPAN * rows
    pairs = [(k_at[p], dk_buf.at[p]) for p in range(PAIR)]
    pairs += [(v_at[p], dv_buf.at[p]) for p in range(PAIR)]
    for at, buf in pairs:
        for j, out in enumerate((d0_ref, d1_ref, d2_ref, d3_ref)):
            out[:rows, at] = buf[j * rows : (j + 1) * rows, :].astype(out.dtype)
        for j in range(2):
            mid = start + 2 * few * j
            dp_ref[j * few : (j + 1) * few, at] = buf[mid : mid + few, :]
            d3_ref[rows + j * few : rows + (j + 1) * few, at] = buf[mid + few : mid + 2 * few, :]
        mid = start + 4 * few
        dp_ref[2 * few :, at] = buf[mid : mid + half, :]
        d3_ref[rows + 2 * few :, at] = buf[mid + half :, :]


def attend(seen, queries, grads, cosine, sine, blocks, prompts):
    rows = queries.shape[0]
    wide = blocks[0].shape[1]
    few, half = prompts[0].shape[0], prompts[2].shape[0] // 2
    keys = SPAN * rows + 4 * few + 2 * half
    part = half + 2 * few
    head = pl.BlockSpec((rows, PAIR * GROUP * HD), lambda i, s: (0, i))
    outs = [(rows, f32), (rows, bf16), (rows, f32), (rows + part, f32), (part, f32)]
    return pl.pallas_call(
        attend_kernel,
        grid_spec=pltpu.PrefetchScalarGridSpec(
            num_scalar_prefetch=1,
            grid=(KVH // PAIR,),
            in_specs=[head, head] + [IN_VMEM] * 9,
            out_specs=[head, head] + [IN_VMEM] * 5,
            scratch_shapes=[pltpu.VMEM((PAIR, keys, HD), bf16)] * 2
            + [pltpu.VMEM((PAIR, keys, HD), f32)] * 2
            + [pltpu.VMEM((2 * part, HD), f32)],
        ),
        out_shape=[jax.ShapeDtypeStruct(queries.shape, bf16)] * 2
        + [jax.ShapeDtypeStruct((r, wide), t) for r, t in outs],
        compiler_params=pltpu.CompilerParams(vmem_limit_bytes=40 * 2**20),
        name="attend",
    )(seen, in_hbm(queries), in_hbm(grads), cosine, sine, *blocks, *prompts)


def merge_kernel(d2_ref, r3_ref, dp_ref, xk_ref, xv_ref, keep_ref, *outs):
    rows, few = d2_ref.shape[0], keep_ref.shape[0]
    x2 = (d2_ref[...] + r3_ref[:rows, :]).astype(bf16)
    xk_ref[:rows, :] = x2[:, :WIDTH]
    xv_ref[:rows, :] = x2[:, WIDTH:]
    keep_ref[...] = dp_ref[:few, :] + r3_ref[rows : rows + few, :]
    near = dp_ref[few : 2 * few, :] + r3_ref[rows + few : rows + 2 * few, :]
    high = near.astype(bf16).astype(f32)
    pair = jnp.concatenate([high, near - high], axis=0).astype(bf16)
    xk_ref[rows:, :] = pair[:, :WIDTH]
    xv_ref[rows:, :] = pair[:, WIDTH:]
    for j, out in enumerate(outs):
        step = out.shape[0]
        at = 2 * few + j * step
        out[...] = dp_ref[at : at + step, :] + r3_ref[rows + at : rows + at + step, :]


def merge(d2, r3, dp, few, pieces):
    rows, wide = d2.shape
    return pl.pallas_call(
        merge_kernel,
        in_specs=[IN_VMEM] * 3,
        out_specs=[IN_VMEM] * (3 + pieces),
        out_shape=[
            jax.ShapeDtypeStruct((rows + 2 * few, WIDTH), bf16),
            jax.ShapeDtypeStruct((rows + 2 * few, WIDTH), bf16),
            jax.ShapeDtypeStruct((few, wide), f32),
        ]
        + [jax.ShapeDtypeStruct((2 * few, wide), f32)] * pieces,
        compiler_params=pltpu.CompilerParams(vmem_limit_bytes=6 * 2**20),
        name="merge",
    )(d2, r3, dp)


def tally_kernel(after_ref, later_ref, *refs):
    terms, keep_ref, send_ref = refs[:-2], refs[-2], refs[-1]
    few = keep_ref.shape[0]
    total = terms[0][...]
    for term in terms[1:]:
        total = total + term[...]
    keep_ref[...] = total[:few]
    send_ref[...] = total[few:]


def tally(after, later, terms):
    few, wide = terms[0].shape
    return pl.pallas_call(
        tally_kernel,
        in_specs=[IN_VMEM] * (2 + len(terms)),
        out_specs=[IN_VMEM] * 2,
        out_shape=[jax.ShapeDtypeStruct((few // 2, wide), f32)] * 2,
        compiler_params=pltpu.CompilerParams(vmem_limit_bytes=2 * 2**20),
        name="tally",
    )(after, later, *terms)


def finish_kernel(
    d0_ref, r1_ref, rk_ref, rv_ref, cos_ref, sin_ref, keep_ref, sum_ref, got_ref,
    gk_ref, gv_ref, gpk_ref, gpv_ref,
):
    rows = d0_ref.shape[0]
    cosine, sine = cos_ref[:rows, :], -sin_ref[:rows, :]
    few = keep_ref.shape[0]
    mine = slice(SPAN * rows, SPAN * rows + 2 * few)
    pcos, psin = cos_ref[mine, :][:few], -sin_ref[mine, :][:few]
    for h in range(KVH):
        at = slice(h * HD, (h + 1) * HD)
        vat = slice(WIDTH + h * HD, WIDTH + (h + 1) * HD)
        for cols, r2_ref, out in ((at, rk_ref, gk_ref), (vat, rv_ref, gv_ref)):
            total = d0_ref[:, cols] + (r1_ref[:, cols].astype(f32) + r2_ref[:rows, at].astype(f32))
            out[:, at] = (turn(total, cosine, sine) if out is gk_ref else total).astype(bf16)
        for cols, r2_ref, out in ((at, rk_ref, gpk_ref), (vat, rv_ref, gpv_ref)):
            pair = r2_ref[rows:, at].astype(f32)
            total = keep_ref[:, cols] + (pair[:few] + pair[few:])
            total = total + (sum_ref[:, cols] + got_ref[:, cols])
            out[:, at] = (turn(total, pcos, psin) if out is gpk_ref else total).astype(bf16)


def finish(d0, r1, rk, rv, cosine, sine, keep, tallied, got):
    rows, few = d0.shape[0], keep.shape[0]
    return pl.pallas_call(
        finish_kernel,
        in_specs=[IN_VMEM] * 9,
        out_shape=[jax.ShapeDtypeStruct((r, WIDTH), bf16) for r in (rows, rows, few, few)],
        compiler_params=pltpu.CompilerParams(vmem_limit_bytes=6 * 2**20),
        name="finish",
    )(d0, r1, rk, rv, cosine, sine, keep, tallied, got)


def local(
    queries, answer_keys, answer_values, prompt_keys, prompt_values, positions, ancestry, out_grad
):
    n = lax.axis_size("ctx")
    chips = n // 2
    rows = queries.shape[0]
    few = prompt_keys.shape[0]
    me = lax.axis_index("ctx")
    core = me & 1
    swap = [(i, i ^ 1) for i in range(n)]
    ahead = [(i, (i + 2) % n) for i in range(n)]
    across = [(i, i + 1) for i in range(0, n, 2)] + [(i, i + 3) for i in range(1, n - 3, 2)]
    turns = chips // 2 - 1
    reach = [(1 + j, 1 + j + turns) for j in range(1, turns + 1)]
    rounds = [[(i, (i + 2 * k[i % 2]) % n) for i in range(n)] for k in reach]

    own, mine = pack(answer_keys, answer_values, prompt_keys, prompt_values)
    w2 = permute(own, ahead)
    theirs = permute(mine, swap)
    chip = jnp.concatenate([mine, theirs], axis=0)
    w1 = permute(lax.optimization_barrier((own, chip))[0], across)
    near = jnp.concatenate([permute(chip, pairs) for pairs in rounds], axis=0)
    w3 = permute(w2, swap)
    others = gather(near, permute(near, swap))

    table = ancestry[0]
    column = jnp.arange(table.shape[0], dtype=jnp.int32)[None, :]
    steps = jnp.arange(SPAN, dtype=jnp.int32)
    steps = jnp.where((core == 0) & (steps > 0), SPAN - steps, steps)
    first = me - steps
    seen = jnp.sum(jnp.where(column == first[:, None], table[None, :], 0), axis=1)
    apart = jnp.sum(
        jnp.where((column >= first[:, None]) & (column < me), table[None, :], 0), axis=1
    )
    places = (positions[None, :] - rows * apart[:, None]).reshape(-1)
    low = jnp.array([k[0] for k in reach], dtype=jnp.int32)
    high = jnp.array([k[1] for k in reach], dtype=jnp.int32)
    away = jnp.concatenate(
        [jnp.array([0, 1], jnp.int32), jnp.where(core == 0, low, high), jnp.where(core == 0, high, low)]
    )
    first_core = jnp.concatenate([jnp.full((2 + turns,), core), jnp.full((turns,), 1 - core)])
    homes = 2 * ((me // 2 - away + chips) % chips)
    homes = jnp.stack([homes + first_core, homes + 1 - first_core], axis=1)
    prompt_places = homes[:, :, None] * few + jnp.arange(few, dtype=jnp.int32)
    cosine, sine = angle_tables(jnp.concatenate([places, prompt_places.reshape(-1)]))

    attended, grad_queries, d0, d1, d2, d3, dp = attend(
        seen[1:], queries, out_grad, cosine, sine, [own, w1, w2, w3], [mine, theirs, others]
    )
    r3 = permute(d3, swap)
    r1 = permute(d1, back(across))
    xk, xv, keep, *terms = merge(d2, r3, dp, few, turns)
    rk = permute(xk, back(ahead))
    sums = [permute(t, back(p)) for t, p in zip(terms, rounds)]
    rv = permute(lax.optimization_barrier((xv, r1, rk, *sums))[0], back(ahead))
    tallied, send = tally(r1, rk, sums)
    got = permute(send, swap)
    grad_keys, grad_values, grad_prompt_keys, grad_prompt_values = finish(
        d0, r1, rk, rv, cosine, sine, keep, tallied, got
    )
    return (attended, grad_queries, grad_keys, grad_values, grad_prompt_keys, grad_prompt_values)


def solution(mesh):
    rows = P(("groups", "ctx"), None)
    return jax.shard_map(
        local,
        mesh=mesh,
        in_specs=(rows, rows, rows, rows, rows, P(("groups", "ctx")), rows, rows),
        out_specs=(rows,) * 6,
        check_vma=False,
    )
```
